1024 devices in a mesh: gx: 16 (over y, core), gy: 8 (over x), gz: 8 (over z).
Axes of the slice: x: 8, y: 8, z: 8, core: 2. Of those that a mesh axis runs over, the one named last changes fastest.
Arguments:
- source: float32 [128, 256, 1024], P('gx', 'gy', 'gz'), may hold values from -24 to 24
- conductivity: float32 [128, 256, 1024], P('gx', 'gy', 'gz'), may hold values from 0.2 to 5
Outputs:
- pressure: float32 [128, 256, 1024], P('gx', 'gy', 'gz')
The draws below stay inside these ranges and needn't reach their ends.
All inputs are finite; a program needn't handle non-finite values.
Results may differ from the reference program's by a relative error of at most 0.00002.
Values sent between devices are 32-bit elements; how exact they have to be, the bound alone decides.
No kernel may reach another device: no remote copies, remote signals or barrier semaphores. Data moves between devices by JAX's collectives and lax.ppermute only.
A program may use at most 64 MiB of HBM per device.

```python
import math
import jax
import jax.numpy as jnp
from jax import lax

CX = 8
CY = 32
CZ = 128
NX = 128
NY = 256
NZ = 1024


def block_levels(key, extent, shards, low, top_value):
    gain, own = 1.0, jax.random.fold_in(key, 6)
    for dim, shards_of in shards:
        heights = jnp.exp(jax.random.uniform(jax.random.fold_in(own, dim), (shards_of,), jnp.float32, low / len(shards), top_value / len(shards)))
        gain = gain * jnp.repeat(heights, extent[dim] // shards_of).reshape([-1 if axis == dim else 1 for axis in range(len(extent))])
    return gain


def scatter_about(own_key, dims, width, limit, cuts=(), kind=jnp.bfloat16):
    array = jax.random.normal(own_key, dims, jnp.float32) * width
    if len(cuts) > 0:
        array = block_levels(own_key, dims, cuts, -0.22, 0.18) * array
    return jnp.clip(array, min=-limit, max=limit).astype(kind)


def setup_inputs(seed: int = 0) -> dict:
    key_list = jax.random.split(jax.random.key(seed), 3)
    source = scatter_about(key_list[0], (NX, NY, NZ), 4.0, 24.0, ((0, 16), (1, 8), (2, 8)), jnp.float32)
    conductivity = jnp.clip(jnp.exp(math.log(5.0) - 3.218876 * jax.random.uniform(key_list[1], (NX, NY, NZ), jnp.float32) ** block_levels(key_list[1], (NX, NY, NZ), ((0, 16), (1, 8), (2, 8)), -0.2, 0.2)), 0.2, 5.0)
    return {"source": source, "conductivity": conductivity}


spectrum_top = 1.9
spectrum_low = 0.475
omega_first = 1.0 / ((spectrum_top + spectrum_low) / 2 + (spectrum_top - spectrum_low) / 2 * math.cos(math.pi / 4))
omega_second = 1.0 / ((spectrum_top + spectrum_low) / 2 + (spectrum_top - spectrum_low) / 2 * math.cos(3 * math.pi / 4))
face_pairs = ((0, 1), (0, -1), (1, 1), (1, -1), (2, 1), (2, -1))


def interior(padded):
    return padded[1:-1, 1:-1, 1:-1]


def neighbour(padded, dimension, offset):
    starts = [1, 1, 1]
    limits = [padded.shape[0] - 1, padded.shape[1] - 1, padded.shape[2] - 1]
    starts[dimension] = 1 + offset
    limits[dimension] = padded.shape[dimension] - 1 + offset
    return lax.slice(padded, tuple(starts), tuple(limits))


def diagonal_of(coeff_pad):
    centre = interior(coeff_pad)
    result = jnp.zeros_like(centre)
    for dimension, offset in face_pairs:
        result = result + 0.5 * (centre + neighbour(coeff_pad, dimension, offset))
    return result


def operate(field_pad, coeff_pad):
    centre = interior(coeff_pad)
    values = interior(field_pad)
    result = jnp.zeros_like(centre)
    for dimension, offset in face_pairs:
        weight = 0.5 * (centre + neighbour(coeff_pad, dimension, offset))
        result = result + weight * (values - neighbour(field_pad, dimension, offset))
    return result


def sweep(field, field_pad, coeff_pad, rhs_field, diagonal, omega_value):
    return field + omega_value * (rhs_field - operate(field_pad, coeff_pad)) / diagonal


def restrict_axis(values, dimension):
    cells = (values.shape[dimension] - 2) // 2
    pieces = [lax.slice_in_dim(values, start_cell, start_cell + 2 * cells - 1, stride=2, axis=dimension) for start_cell in range(4)]
    return (pieces[0] + 3.0 * pieces[1] + 3.0 * pieces[2] + pieces[3]) * 0.125


def restrict(padded):
    return restrict_axis(restrict_axis(restrict_axis(padded, 0), 1), 2)


def interpolate_axis(values, dimension):
    cells = values.shape[dimension] - 2
    lower_side = lax.slice_in_dim(values, 0, cells, axis=dimension)
    centre = lax.slice_in_dim(values, 1, cells + 1, axis=dimension)
    upper_side = lax.slice_in_dim(values, 2, cells + 2, axis=dimension)
    even_cells = 0.75 * centre + 0.25 * lower_side
    odd_cells = 0.75 * centre + 0.25 * upper_side
    paired = jnp.stack([even_cells, odd_cells], axis=dimension + 1)
    new_shape = list(values.shape)
    new_shape[dimension] = 2 * cells
    return paired.reshape(tuple(new_shape))


def interpolate(padded):
    return interpolate_axis(interpolate_axis(interpolate_axis(padded, 0), 1), 2)


def coarsen(values):
    first, second, third = values.shape
    return values.reshape(first // 2, 2, second // 2, 2, third // 2, 2).mean(axis=(1, 3, 5))


def pad_zero(values):
    return jnp.pad(values, 1)


def box_correction(coeff_box, rhs_box):
    coeff_pad = pad_zero(coeff_box)
    diagonal = diagonal_of(coeff_pad)
    field = omega_first * rhs_box / diagonal
    field = sweep(field, pad_zero(field), coeff_pad, rhs_box, diagonal, omega_second)
    return interpolate(pad_zero(field))


def split_boxes(values, box_sizes):
    first, second, third = values.shape
    sized = values.reshape(first // box_sizes[0], box_sizes[0], second // box_sizes[1], box_sizes[1], third // box_sizes[2], box_sizes[2])
    return sized.transpose(0, 2, 4, 1, 3, 5).reshape(-1, box_sizes[0], box_sizes[1], box_sizes[2])


def join_boxes(boxes, box_counts):
    inner = boxes.shape[1:]
    sized = boxes.reshape(box_counts[0], box_counts[1], box_counts[2], inner[0], inner[1], inner[2])
    return sized.transpose(0, 3, 1, 4, 2, 5).reshape(box_counts[0] * inner[0], box_counts[1] * inner[1], box_counts[2] * inner[2])


def reference(source, conductivity):
    coeff_pad = pad_zero(conductivity)
    fine_diag = diagonal_of(coeff_pad)
    pressure = omega_first * source / fine_diag
    pressure = sweep(pressure, pad_zero(pressure), coeff_pad, source, fine_diag, omega_second)
    leftover = source - operate(pad_zero(pressure), coeff_pad)
    middle_rhs = 4.0 * restrict(pad_zero(leftover))
    middle_coeff = coarsen(conductivity)
    middle_pad = pad_zero(middle_coeff)
    middle_diag = diagonal_of(middle_pad)
    middle = omega_first * middle_rhs / middle_diag
    middle = sweep(middle, pad_zero(middle), middle_pad, middle_rhs, middle_diag, omega_second)
    middle_left = middle_rhs - operate(pad_zero(middle), middle_pad)
    coarse_rhs = 4.0 * restrict(pad_zero(middle_left))
    coarse_coeff = coarsen(middle_coeff)
    box_sizes = (CX // 2, CY // 2, CZ // 2)
    box_counts = tuple(coarse_coeff.shape[place] // box_sizes[place] for place in range(3))
    corrections = jax.vmap(box_correction)(split_boxes(coarse_coeff, box_sizes), split_boxes(coarse_rhs, box_sizes))
    middle = middle + join_boxes(corrections, box_counts)
    for omega_value in (omega_first, omega_second):
        middle = sweep(middle, pad_zero(middle), middle_pad, middle_rhs, middle_diag, omega_value)
    pressure = pressure + interpolate(pad_zero(middle))
    for omega_value in (omega_first, omega_second):
        pressure = sweep(pressure, pad_zero(pressure), coeff_pad, source, fine_diag, omega_value)
    return pressure
```

```python
import math

import jax
import jax.numpy as jnp
from jax import lax
from jax.sharding import PartitionSpec as P

spectrum_top = 1.9
spectrum_low = 0.475
mean_value = (spectrum_top + spectrum_low) / 2
half_range = (spectrum_top - spectrum_low) / 2
omega_first = 1.0 / (mean_value + half_range * math.cos(math.pi / 4))
omega_second = 1.0 / (mean_value + half_range * math.cos(3 * math.pi / 4))
HIGHEST = lax.Precision.HIGHEST


def swap(block, axis, outer):
    count = lax.axis_size(axis)
    route = []
    for low in range(1 if outer else 0, count - 1, 2):
        route += [(low, low + 1), (low + 1, low)]
    return lax.ppermute(block, axis, route)


def cut(values, start, stop, dim):
    return lax.slice_in_dim(values, start, stop, axis=dim)


def join(pieces, dim):
    return jnp.concatenate(pieces, axis=dim)


def ahead(values, dim):
    return jnp.roll(values, -1, dim)


def behind(values, dim):
    return jnp.roll(values, 1, dim)


def weights(coeff):
    faces = [0.5 * (coeff + ahead(coeff, dim)) for dim in range(3)]
    diagonal = sum(faces[dim] + behind(faces[dim], dim) for dim in range(3))
    inside = coeff > 0
    inverse = jnp.where(inside, 1.0 / jnp.where(inside, diagonal, 1.0), 0.0)
    return faces, inverse


def operate(field, faces):
    result = 0.0
    for dim in range(3):
        flux = faces[dim] * (field - ahead(field, dim))
        result = result + flux - behind(flux, dim)
    return result


def sweep(field, faces, inverse, rhs, omega):
    return field + omega * (rhs - operate(field, faces)) * inverse


def pre_smooth(faces, inverse, rhs):
    return sweep(omega_first * rhs * inverse, faces, inverse, rhs, omega_second)


def lane_map(rows, columns, entries):
    row = lax.broadcasted_iota(jnp.int32, (rows, columns), 0)
    column = lax.broadcasted_iota(jnp.int32, (rows, columns), 1)
    return entries(row, column).astype(jnp.float32)


def signed(index, size, after):
    return jnp.where(index < after, index, index - size)


def gather_weights(fine, coarse):
    step = fine - 2 * coarse
    return jnp.where((step == 0) | (step == 1), 0.375, jnp.where((step == -1) | (step == 2), 0.125, 0.0))


def mean_weights(fine, coarse):
    step = fine - 2 * coarse
    return jnp.where((step == 0) | (step == 1), 0.5, 0.0)


def spread_weights(coarse, fine):
    step = fine - 2 * coarse
    return jnp.where((step == 0) | (step == 1), 0.75, jnp.where((step == -1) | (step == 2), 0.25, 0.0))


def lanes_dot(values, matrix):
    return lax.dot_general(values, matrix, (((2,), (0,)), ((), ())), precision=HIGHEST)


def halves(values, dim):
    size = values.shape[dim]
    even = lax.slice_in_dim(values, 0, size - 1, stride=2, axis=dim)
    odd = lax.slice_in_dim(values, 1, size, stride=2, axis=dim)
    return even, odd


def restrict_two(values):
    for dim in (0, 1):
        even, odd = halves(values, dim)
        values = 0.375 * (even + odd) + 0.125 * (behind(odd, dim) + ahead(even, dim))
    return values


def mean_two(values):
    for dim in (0, 1):
        even, odd = halves(values, dim)
        values = 0.5 * (even + odd)
    return values


def spread_axis(values, dim):
    even = 0.75 * values + 0.25 * behind(values, dim)
    odd = 0.75 * values + 0.25 * ahead(values, dim)
    paired = jnp.stack([even, odd], axis=dim + 1)
    shape = list(values.shape)
    shape[dim] *= 2
    return paired.reshape(tuple(shape))


def take_lanes(values, matrix):
    rows = values.reshape(-1, values.shape[-1])
    return lax.dot_general(matrix, rows, (((0,), (1,)), ((), ())), precision=HIGHEST)


def put_lanes(strip, matrix, shape):
    rows = lax.dot_general(strip, matrix, (((0,), (0,)), ((), ())), precision=HIGHEST)
    return rows.reshape(shape)


def local(source, conductivity):
    low_x = lax.axis_index("gx") % 2 == 0
    low_y = lax.axis_index("gy") % 2 == 0
    low_z = lax.axis_index("gz") % 2 == 0

    def side(low, when_low, when_high):
        return jnp.where(low, when_low, when_high)

    cells = jnp.stack([source, conductivity])
    near = swap(side(low_x, cells[:, 4:], cells[:, :4]), "gx", False)
    far = swap(side(low_x, join([cells, near[:, :2]], 1), join([near[:, 2:], cells], 1)), "gx", True)
    cells = join([cells, side(low_x, join([near, far], 1), join([far, near], 1))], 1)

    near = swap(side(low_y, cells[:, :, 28:], cells[:, :, :4]), "gy", False)
    far = swap(side(low_y, cells[:, :, :12], cells[:, :, 20:]), "gy", True)
    cells = join([cells, side(low_y, join([near, far], 2), join([far, near], 2))], 2)

    base_near = side(low_z, 124, 0)
    base_far = side(low_z, 0, 118)
    near = swap(take_lanes(cells, lane_map(128, 4, lambda z, k: z == k + base_near)), "gz", False)
    far = swap(take_lanes(cells, lane_map(128, 10, lambda z, k: z == k + base_far)), "gz", True)
    to_near = side(low_z, 0, 124)
    to_far = side(low_z, 118, 0)
    added = put_lanes(near, lane_map(4, 128, lambda k, z: z == k + to_near), (2, 22, 48, 128))
    added = added + put_lanes(far, lane_map(10, 128, lambda k, z: z == k + to_far), (2, 22, 48, 128))
    source_wide, coeff = join([cells, added], 3)

    faces, inverse = weights(coeff)
    pre_pressure = pre_smooth(faces, inverse, source_wide)
    leftover = jnp.where(coeff > 0, source_wide - operate(pre_pressure, faces), 0.0)
    to_middle = lane_map(256, 128, lambda f, c: gather_weights(signed(f, 256, 192), signed(c, 128, 96)))
    mean_middle = lane_map(256, 128, lambda f, c: mean_weights(signed(f, 256, 192), signed(c, 128, 96)))
    middle_rhs = 4.0 * lanes_dot(restrict_two(leftover), to_middle)
    middle_coeff = lanes_dot(mean_two(coeff), mean_middle)

    pair = jnp.stack([middle_rhs, middle_coeff])
    base_near = side(low_z, 52, 0)
    to_near = side(low_z, 64, 116)
    near = swap(take_lanes(pair, lane_map(128, 12, lambda z, k: z == k + base_near)), "gz", False)
    lane = lax.broadcasted_iota(jnp.int32, (1, 1, 1, 128), 3)
    kept = (lane < 64) | side(low_z, lane >= 124, lane < 68)
    pair = jnp.where(kept, pair, put_lanes(near, lane_map(12, 128, lambda k, z: z == k + to_near), pair.shape))

    near = swap(side(low_y, pair[:, :, 4:16], pair[:, :, :12]), "gy", False)
    pair = side(
        low_y,
        join([pair[:, :, :16], near, pair[:, :, 20:]], 2),
        join([pair[:, :, :20], near], 2),
    )
    near = swap(side(low_x, join([pair[:, 7:], pair[:, :4]], 1), pair[:, :8]), "gx", False)
    middle_rhs, middle_coeff = side(
        low_x, join([pair[:, :4], near, pair[:, 7:]], 1), join([pair[:, :8], near], 1)
    )

    faces_m, inverse_m = weights(middle_coeff)
    middle = pre_smooth(faces_m, inverse_m, middle_rhs)
    middle_left = jnp.where(middle_coeff > 0, middle_rhs - operate(middle, faces_m), 0.0)

    def coarse_lane(c):
        return signed(c, 128, 48)

    def middle_lane(m):
        return signed(m, 128, 96)

    to_coarse = lane_map(128, 128, lambda m, c: gather_weights(middle_lane(m), coarse_lane(c)))
    mean_coarse = lane_map(128, 128, lambda m, c: mean_weights(middle_lane(m), coarse_lane(c)))
    from_coarse = lane_map(128, 128, lambda c, m: spread_weights(coarse_lane(c), middle_lane(m)))
    place = [lax.broadcasted_iota(jnp.int32, (8, 16, 128), dim) for dim in range(3)]
    in_box = (
        side(low_x, place[0] < 4, (place[0] < 2) | (place[0] >= 6))
        & side(low_y, place[1] < 14, (place[1] < 8) | (place[1] >= 10))
        & side(low_z, place[2] < 64, (place[2] < 32) | (place[2] >= 64))
    )
    coarse_rhs = jnp.where(in_box, 4.0 * lanes_dot(restrict_two(middle_left), to_coarse), 0.0)
    coarse_coeff = jnp.where(in_box, lanes_dot(mean_two(middle_coeff), mean_coarse), 0.0)
    faces_c, inverse_c = weights(coarse_coeff)
    coarse = pre_smooth(faces_c, inverse_c, coarse_rhs)
    correction = spread_axis(spread_axis(lanes_dot(coarse, from_coarse), 0), 1)
    middle = middle + correction

    def trim(values):
        values = join([values[:8], values[12:]], 0)
        return join([values[:, :20], values[:, 28:]], 1)

    middle = trim(middle)
    base_far = side(low_z, 0, 60)
    to_far = side(low_z, 124, 64)
    far = swap(take_lanes(middle, lane_map(128, 4, lambda z, k: z == k + base_far)), "gz", True)
    lane = lane[0]
    taken = side(low_z, lane >= 124, (lane >= 64) & (lane < 68))
    middle = jnp.where(taken, put_lanes(far, lane_map(4, 128, lambda k, z: z == k + to_far), middle.shape), middle)
    far = swap(side(low_y, middle[:, :4], middle[:, 12:16]), "gy", True)
    middle = side(
        low_y, join([middle[:, :20], far], 1), join([middle[:, :16], far, middle[:, 20:]], 1)
    )
    far = swap(side(low_x, middle[:4], middle[:4]), "gx", True)
    middle = side(low_x, join([middle[:8], far], 0), join([middle[:4], far, middle[8:]], 0))

    middle_rhs = trim(middle_rhs)
    faces_m, inverse_m = weights(trim(middle_coeff))
    middle = sweep(middle, faces_m, inverse_m, middle_rhs, omega_first)
    middle = sweep(middle, faces_m, inverse_m, middle_rhs, omega_second)

    def narrow(values):
        values = join([values[:10], values[20:]], 0)
        return join([values[:, :36], values[:, 44:]], 1)

    middle = join([middle[:6], middle[10:]], 0)
    middle = join([middle[:, :18], middle[:, 22:]], 1)
    to_fine = lane_map(128, 256, lambda c, f: spread_weights(signed(c, 128, 96), signed(f, 256, 192)))
    risen = spread_axis(spread_axis(lanes_dot(middle, to_fine), 0), 1)
    risen = join([risen[:10], risen[14:]], 0)
    coeff = narrow(coeff)
    source_wide = narrow(source_wide)
    faces, inverse = weights(coeff)
    pressure = narrow(pre_pressure) + jnp.where(coeff > 0, risen, 0.0)
    pressure = sweep(pressure, faces, inverse, source_wide, omega_first)
    pressure = sweep(pressure, faces, inverse, source_wide, omega_second)
    return pressure[:8, :32, :128]


def solution(mesh):
    spec = P("gx", "gy", "gz")
    return jax.shard_map(local, mesh=mesh, in_specs=(spec, spec), out_specs=spec, check_vma=False)
```

```python
import math

import jax
import jax.numpy as jnp
from jax import lax
from jax.experimental import pallas as pl
from jax.experimental.pallas import tpu as pltpu
from jax.sharding import PartitionSpec as P

spectrum_top = 1.9
spectrum_low = 0.475
mean_value = (spectrum_top + spectrum_low) / 2
half_range = (spectrum_top - spectrum_low) / 2
omega_first = 1.0 / (mean_value + half_range * math.cos(math.pi / 4))
omega_second = 1.0 / (mean_value + half_range * math.cos(3 * math.pi / 4))
HIGHEST = lax.Precision.HIGHEST


def swap(block, axis, outer):
    count = lax.axis_size(axis)
    route = []
    for low in range(1 if outer else 0, count - 1, 2):
        route += [(low, low + 1), (low + 1, low)]
    return lax.ppermute(block, axis, route)


def cut(values, start, stop, dim):
    return lax.slice_in_dim(values, start, stop, axis=dim)


def join(pieces, dim):
    return jnp.concatenate(pieces, axis=dim)


def turn(plane, dim, step):
    return pltpu.roll(plane, -step % plane.shape[dim], dim)


class Operator:
    def __init__(self, count, faces):
        self.count = count
        self.faces = faces

    def build(self, coeff, take):
        before = 0.5 * (coeff(self.count - 1) + coeff(0))
        for i in range(self.count):
            here = coeff(i)
            across = 0.5 * (here + coeff((i + 1) % self.count))
            rows = 0.5 * (here + turn(here, 0, 1))
            lanes = 0.5 * (here + turn(here, 1, 1))
            for place, face in enumerate((across, rows, lanes)):
                self.faces[place, i] = face
            diagonal = (across + before) + (rows + turn(rows, 0, -1)) + (lanes + turn(lanes, 1, -1))
            inside = here > 0
            take(i, jnp.where(inside, 1.0 / jnp.where(inside, diagonal, 1.0), 0.0))
            before = across

    def apply(self, field, take):
        last = self.count - 1
        before = self.faces[0, last] * (field[last] - field[0])
        for i in range(self.count):
            here = field[i]
            across = self.faces[0, i] * (here - field[(i + 1) % self.count])
            rows = self.faces[1, i] * (here - turn(here, 0, 1))
            lanes = self.faces[2, i] * (here - turn(here, 1, 1))
            take(i, (across - before) + (rows - turn(rows, 0, -1)) + (lanes - turn(lanes, 1, -1)))
            before = across


def sweep(operator, field, inverse, rhs, omega, store):
    def take(i, applied):
        store(i, field[i] + (omega * (rhs(i) - applied)) * inverse[i])

    operator.apply(field, take)


def halve_rows(piece, weights):
    count = piece.shape[0] // 2
    even = piece[pl.ds(0, count, 2), :]
    odd = piece[pl.ds(1, count, 2), :]
    if not weights:
        return even + odd
    return 0.375 * (even + odd) + 0.125 * (turn(odd, 0, -1) + turn(even, 0, 1))


def product(values, matrix):
    return jnp.dot(values, matrix, precision=HIGHEST, preferred_element_type=jnp.float32)


def lane_map(rows, columns, entries):
    row = lax.broadcasted_iota(jnp.int32, (rows, columns), 0)
    column = lax.broadcasted_iota(jnp.int32, (rows, columns), 1)
    return entries(row, column).astype(jnp.float32)


def signed(index, size, after):
    return jnp.where(index < after, index, index - size)


def gather_weights(fine, coarse):
    step = fine - 2 * coarse
    return jnp.where((step == 0) | (step == 1), 0.375, jnp.where((step == -1) | (step == 2), 0.125, 0.0))


def mean_weights(fine, coarse):
    step = fine - 2 * coarse
    return jnp.where((step == 0) | (step == 1), 0.5, 0.0)


def spread_weights(coarse, fine):
    step = fine - 2 * coarse
    return jnp.where((step == 0) | (step == 1), 0.75, jnp.where((step == -1) | (step == 2), 0.25, 0.0))


def fine_lane(f):
    return signed(f, 256, 192)


def middle_lane(m):
    return signed(m, 128, 96)


def coarse_lane(c):
    return signed(c, 128, 48)


def fine_plane(cells, added, kind, i):
    return jnp.concatenate([cells[kind, i], added[kind, i]], axis=1)


def restrict_planes(plane, j, count):
    return 0.375 * (plane[2 * j] + plane[2 * j + 1]) + 0.125 * (
        plane[(2 * j - 1) % count] + plane[(2 * j + 2) % count]
    )


def fine_kernel(cells, added, pair, pressure, faces, inverse, field, other, piece, packed):
    def coeff(i):
        return fine_plane(cells, added, 1, i)

    def rhs(i):
        return fine_plane(cells, added, 0, i)

    operator = Operator(22, faces)

    def begin(i, value):
        inverse[i] = value
        field[i] = omega_first * rhs(i) * value

    operator.build(coeff, begin)

    def store(i, value):
        other[i] = value
        if i < 10:
            pressure[i] = value
        elif i >= 20:
            pressure[i - 10] = value

    sweep(operator, field, inverse, rhs, omega_second, store)

    def leave(i, applied):
        field[i] = jnp.where(coeff(i) > 0, rhs(i) - applied, 0.0)

    operator.apply(other, leave)
    for j in range(11):
        planes = (restrict_planes(field, j, 22), coeff(2 * j) + coeff(2 * j + 1))
        for kind in range(2):
            for half in range(2):
                slot = piece.at[(2 * j + kind) * 2 + half]
                slot[...] = planes[kind][:, 128 * half : 128 * half + 128]
                packed[kind, pl.ds(24 * j, 24), pl.ds(128 * half, 128)] = halve_rows(slot, kind == 0)
    matrices = (
        lane_map(256, 128, lambda f, c: 4.0 * gather_weights(fine_lane(f), middle_lane(c))),
        lane_map(256, 128, lambda f, c: 0.25 * mean_weights(fine_lane(f), middle_lane(c))),
    )
    for kind in range(2):
        result = product(packed[kind], matrices[kind])
        for j in range(11):
            pair[kind, j] = result[24 * j : 24 * j + 24]


def box_kernel(pair, box, corrected, faces, inverse, field, other, piece, packed, low, low_faces, low_inverse, risen):
    def coeff(i):
        return pair[1, i]

    def rhs(i):
        return pair[0, i]

    operator = Operator(16, faces)

    def begin(i, value):
        inverse[i] = value
        field[i] = omega_first * rhs(i) * value

    operator.build(coeff, begin)

    def store(i, value):
        other[i] = value

    sweep(operator, field, inverse, rhs, omega_second, store)

    def leave(i, applied):
        field[i] = jnp.where(coeff(i) > 0, rhs(i) - applied, 0.0)

    operator.apply(other, leave)
    for j in range(8):
        planes = (restrict_planes(field, j, 16), coeff(2 * j) + coeff(2 * j + 1))
        for kind in range(2):
            slot = piece.at[2 * j + kind]
            slot[...] = planes[kind]
            packed[kind, pl.ds(16 * j, 16), :] = halve_rows(slot, kind == 0)
    matrices = (
        lane_map(128, 128, lambda m, c: 4.0 * gather_weights(middle_lane(m), coarse_lane(c))),
        lane_map(128, 128, lambda m, c: 0.25 * mean_weights(middle_lane(m), coarse_lane(c))),
    )
    for kind in range(2):
        result = product(packed[kind], matrices[kind])
        for j in range(8):
            low[kind, j] = result[16 * j : 16 * j + 16] * box[j]

    coarse = Operator(8, low_faces)

    def begin_low(i, value):
        low_inverse[i] = value
        low[2, i] = omega_first * low[0, i] * value

    coarse.build(lambda i: low[1, i], begin_low)

    def store_low(i, value):
        packed[0, pl.ds(16 * i, 16), :] = value

    sweep(coarse, low.at[2], low_inverse, lambda i: low[0, i], omega_second, store_low)
    result = product(
        packed[0], lane_map(128, 128, lambda c, m: spread_weights(coarse_lane(c), middle_lane(m)))
    )
    for j in range(8):
        spread_rows(result[16 * j : 16 * j + 16], risen.at[j])
    for place in range(12):
        i = place if place < 8 else place + 4
        near = (i // 2 + (1 if i % 2 else -1)) % 8
        corrected[place] = other[i] + (0.75 * risen[i // 2] + 0.25 * risen[near])


def spread_rows(values, target):
    count = values.shape[0]
    target[pl.ds(0, count, 2), :] = 0.75 * values + 0.25 * turn(values, 0, -1)
    target[pl.ds(1, count, 2), :] = 0.75 * values + 0.25 * turn(values, 0, 1)


def last_kernel(middle, pair, cells, added, pre, out, faces, inverse, field, faces_m, inverse_m, field_m, packed, risen):
    def coeff_m(i):
        return pair[1, i if i < 8 else i + 4]

    def rhs_m(i):
        return pair[0, i if i < 8 else i + 4]

    operator = Operator(12, faces_m)

    def keep_m(i, value):
        inverse_m[i] = value

    operator.build(coeff_m, keep_m)

    def store_m(i, value):
        field_m[i] = value

    sweep(operator, middle, inverse_m, rhs_m, omega_first, store_m)

    def store_packed(i, value):
        place = (i + 2) % 12
        if place < 8:
            packed[pl.ds(32 * place, 32), :] = value

    sweep(operator, field_m, inverse_m, rhs_m, omega_second, store_packed)

    def coeff(i):
        return fine_plane(cells, added, 1, i if i < 10 else i + 10)

    def rhs(i):
        return fine_plane(cells, added, 0, i if i < 10 else i + 10)

    fine = Operator(12, faces)

    def keep(i, value):
        inverse[i] = value

    fine.build(coeff, keep)
    result = product(
        packed[...], lane_map(128, 256, lambda c, f: spread_weights(middle_lane(c), fine_lane(f)))
    )
    for place in range(8):
        for half in range(2):
            spread_rows(
                result[32 * place : 32 * place + 32, 128 * half : 128 * half + 128],
                risen.at[2 * place + half],
            )

    def lifted(place):
        halves = [
            jnp.concatenate([risen[2 * place + half, 0:40], risen[2 * place + half, 56:64]], axis=0)
            for half in range(2)
        ]
        return jnp.concatenate(halves, axis=1)

    for i in range(12):
        fine_index = i if i < 10 else i - 12
        place = fine_index // 2 + 2
        near = place + (1 if fine_index % 2 else -1)
        value = 0.75 * lifted(place) + 0.25 * lifted(near)
        field[0, i] = pre[i] + jnp.where(coeff(i) > 0, value, 0.0)

    def store(i, value):
        field[1, i] = value

    sweep(fine, field.at[0], inverse, rhs, omega_first, store)

    def store_out(i, value):
        if i < 8:
            out[i] = value[:32, :128]

    sweep(fine, field.at[1], inverse, rhs, omega_second, store_out)


interpret = False
VMEM = pl.BlockSpec(memory_space=pltpu.VMEM)


def call(kernel, outs, scratch, *arguments):
    return pl.pallas_call(
        kernel,
        out_shape=[jax.ShapeDtypeStruct(shape, jnp.float32) for shape in outs],
        in_specs=[VMEM] * len(arguments),
        out_specs=[VMEM] * len(outs),
        scratch_shapes=[pltpu.VMEM(shape, jnp.float32) for shape in scratch],
        compiler_params=pltpu.CompilerParams(vmem_limit_bytes=24 * 1024 * 1024),
        interpret=interpret,
    )(*arguments)


def take_lanes(values, matrix):
    rows = values.reshape(-1, values.shape[-1])
    return lax.dot_general(matrix, rows, (((0,), (1,)), ((), ())), precision=HIGHEST)


def put_lanes(strip, matrix, shape):
    rows = lax.dot_general(strip, matrix, (((0,), (0,)), ((), ())), precision=HIGHEST)
    return rows.reshape(shape)


def local(source, conductivity):
    low_x = lax.axis_index("gx") % 2 == 0
    low_y = lax.axis_index("gy") % 2 == 0
    low_z = lax.axis_index("gz") % 2 == 0

    def side(low, when_low, when_high):
        return jnp.where(low, when_low, when_high)

    cells = jnp.stack([source, conductivity])
    near = swap(side(low_x, cells[:, 4:], cells[:, :4]), "gx", False)
    far = swap(side(low_x, join([cells, near[:, :2]], 1), join([near[:, 2:], cells], 1)), "gx", True)
    cells = join([cells, side(low_x, join([near, far], 1), join([far, near], 1))], 1)

    near = swap(side(low_y, cells[:, :, 28:], cells[:, :, :4]), "gy", False)
    far = swap(side(low_y, cells[:, :, :12], cells[:, :, 20:]), "gy", True)
    cells = join([cells, side(low_y, join([near, far], 2), join([far, near], 2))], 2)

    base_near = side(low_z, 124, 0)
    base_far = side(low_z, 0, 118)
    near = swap(take_lanes(cells, lane_map(128, 4, lambda z, k: z == k + base_near)), "gz", False)
    far = swap(take_lanes(cells, lane_map(128, 10, lambda z, k: z == k + base_far)), "gz", True)
    to_near = side(low_z, 0, 124)
    to_far = side(low_z, 118, 0)
    added = put_lanes(near, lane_map(4, 128, lambda k, z: z == k + to_near), (2, 22, 48, 128))
    added = added + put_lanes(far, lane_map(10, 128, lambda k, z: z == k + to_far), (2, 22, 48, 128))

    plane = (48, 256)
    pair, pre_pressure = call(
        fine_kernel,
        [(2, 11, 24, 128), (12, *plane)],
        [(3, 22, *plane), (22, *plane), (22, *plane), (22, *plane), (44, 48, 128), (2, 264, 256)],
        cells,
        added,
    )

    base_near = side(low_z, 52, 0)
    to_near = side(low_z, 64, 116)
    near = swap(take_lanes(pair, lane_map(128, 12, lambda z, k: z == k + base_near)), "gz", False)
    lane = lax.broadcasted_iota(jnp.int32, (1, 1, 1, 128), 3)
    kept = (lane < 64) | side(low_z, lane >= 124, lane < 68)
    pair = jnp.where(kept, pair, put_lanes(near, lane_map(12, 128, lambda k, z: z == k + to_near), pair.shape))

    near = swap(side(low_y, pair[:, :, 4:16], pair[:, :, :12]), "gy", False)
    pair = side(
        low_y,
        join([pair[:, :, :16], near, pair[:, :, 20:]], 2),
        join([pair[:, :, :20], near], 2),
    )
    near = swap(side(low_x, join([pair[:, 7:], pair[:, :4]], 1), pair[:, :8]), "gx", False)
    pair = side(low_x, join([pair[:, :4], near, pair[:, 7:]], 1), join([pair[:, :8], near], 1))

    place = [lax.broadcasted_iota(jnp.int32, (8, 16, 128), dim) for dim in range(3)]
    in_box = (
        side(low_x, place[0] < 4, (place[0] < 2) | (place[0] >= 6))
        & side(low_y, place[1] < 14, (place[1] < 8) | (place[1] >= 10))
        & side(low_z, place[2] < 64, (place[2] < 32) | (place[2] >= 64))
    )
    (middle,) = call(
        box_kernel,
        [(12, 32, 128)],
        [(3, 16, 32, 128), (16, 32, 128), (16, 32, 128), (16, 32, 128), (16, 32, 128), (2, 128, 128)]
        + [(3, 8, 16, 128), (3, 8, 16, 128), (8, 16, 128), (8, 32, 128)],
        pair,
        in_box.astype(jnp.float32),
    )

    base_far = side(low_z, 0, 60)
    to_far = side(low_z, 124, 64)
    far = swap(take_lanes(middle, lane_map(128, 4, lambda z, k: z == k + base_far)), "gz", True)
    lane = lane[0]
    taken = side(low_z, lane >= 124, (lane >= 64) & (lane < 68))
    middle = jnp.where(taken, put_lanes(far, lane_map(4, 128, lambda k, z: z == k + to_far), middle.shape), middle)
    far = swap(side(low_y, middle[:, :4], middle[:, 12:16]), "gy", True)
    middle = side(
        low_y, join([middle[:, :28], far], 1), join([middle[:, :16], far, middle[:, 20:]], 1)
    )
    far = swap(side(low_x, middle[:4], middle[:4]), "gx", True)
    middle = side(low_x, join([middle[:8], far], 0), join([middle[:4], far, middle[8:]], 0))

    (pressure,) = call(
        last_kernel,
        [(8, 32, 128)],
        [(3, 12, *plane), (12, *plane), (2, 12, *plane), (3, 12, 32, 128), (12, 32, 128), (12, 32, 128)]
        + [(256, 128), (16, 64, 128)],
        middle,
        pair,
        cells,
        added,
        pre_pressure,
    )
    return pressure


def solution(mesh):
    spec = P("gx", "gy", "gz")
    return jax.shard_map(local, mesh=mesh, in_specs=(spec, spec), out_specs=spec, check_vma=False)
```

```python
import math

import jax
import jax.numpy as jnp
from jax import lax
from jax.experimental import pallas as pl
from jax.experimental.pallas import tpu as pltpu
from jax.sharding import PartitionSpec as P

spectrum_top = 1.9
spectrum_low = 0.475
mean_value = (spectrum_top + spectrum_low) / 2
half_range = (spectrum_top - spectrum_low) / 2
omega_first = 1.0 / (mean_value + half_range * math.cos(math.pi / 4))
omega_second = 1.0 / (mean_value + half_range * math.cos(3 * math.pi / 4))
HIGHEST = lax.Precision.HIGHEST


def swap(block, axis, outer):
    count = lax.axis_size(axis)
    route = []
    for low in range(1 if outer else 0, count - 1, 2):
        route += [(low, low + 1), (low + 1, low)]
    return lax.ppermute(block, axis, route)


def cut(values, start, stop, dim):
    return lax.slice_in_dim(values, start, stop, axis=dim)


def join(pieces, dim):
    return jnp.concatenate(pieces, axis=dim)


def turn(plane, dim, step):
    return pltpu.roll(plane, -step % plane.shape[dim], dim)


class Operator:
    def __init__(self, count, faces):
        self.count = count
        self.faces = faces

    def build(self, coeff, take):
        before = 0.5 * (coeff(self.count - 1) + coeff(0))
        for i in range(self.count):
            here = coeff(i)
            across = 0.5 * (here + coeff((i + 1) % self.count))
            rows = 0.5 * (here + turn(here, 0, 1))
            lanes = 0.5 * (here + turn(here, 1, 1))
            for place, face in enumerate((across, rows, lanes)):
                self.faces[place, i] = face
            diagonal = (across + before) + (rows + turn(rows, 0, -1)) + (lanes + turn(lanes, 1, -1))
            inside = here > 0
            take(i, jnp.where(inside, 1.0 / jnp.where(inside, diagonal, 1.0), 0.0))
            before = across

    def apply(self, field, take):
        last = self.count - 1
        before = self.faces[0, last] * (field[last] - field[0])
        for i in range(self.count):
            here = field[i]
            across = self.faces[0, i] * (here - field[(i + 1) % self.count])
            rows = self.faces[1, i] * (here - turn(here, 0, 1))
            lanes = self.faces[2, i] * (here - turn(here, 1, 1))
            take(i, (across - before) + (rows - turn(rows, 0, -1)) + (lanes - turn(lanes, 1, -1)))
            before = across


def sweep(operator, field, inverse, rhs, omega, store):
    def take(i, applied):
        store(i, field[i] + (omega * (rhs(i) - applied)) * inverse[i])

    operator.apply(field, take)


def halve_rows(piece, weights):
    count = piece.shape[0] // 2
    even = piece[pl.ds(0, count, 2), :]
    odd = piece[pl.ds(1, count, 2), :]
    if not weights:
        return even + odd
    return 0.375 * (even + odd) + 0.125 * (turn(odd, 0, -1) + turn(even, 0, 1))


def product(values, matrix):
    return jnp.dot(values, matrix, precision=HIGHEST, preferred_element_type=jnp.float32)


def lane_map(rows, columns, entries):
    row = lax.broadcasted_iota(jnp.int32, (rows, columns), 0)
    column = lax.broadcasted_iota(jnp.int32, (rows, columns), 1)
    return entries(row, column).astype(jnp.float32)


def signed(index, size, after):
    return jnp.where(index < after, index, index - size)


def gather_weights(fine, coarse):
    step = fine - 2 * coarse
    return jnp.where((step == 0) | (step == 1), 0.375, jnp.where((step == -1) | (step == 2), 0.125, 0.0))


def mean_weights(fine, coarse):
    step = fine - 2 * coarse
    return jnp.where((step == 0) | (step == 1), 0.5, 0.0)


def spread_weights(coarse, fine):
    step = fine - 2 * coarse
    return jnp.where((step == 0) | (step == 1), 0.75, jnp.where((step == -1) | (step == 2), 0.25, 0.0))


def fine_lane(f):
    return signed(f, 256, 192)


def middle_lane(m):
    return signed(m, 128, 96)


def coarse_lane(lane, odd):
    after = jnp.where(lane < 32, lane, jnp.where((lane == 32) & (odd == 1), 4096, lane - odd))
    before = jnp.where((lane == 127) & (odd == 0), 4096, lane - 127 - odd)
    return jnp.where(lane < 64, after, before)


def same_box(coarse, middle, odd):
    edge = 32 * odd
    return (coarse >= edge) == (middle >= 2 * edge)


def fine_plane(cells, added, kind, i):
    return jnp.concatenate([cells[kind, i], added[kind, i]], axis=1)


def restrict_planes(plane, j, count):
    return 0.375 * (plane[2 * j] + plane[2 * j + 1]) + 0.125 * (
        plane[(2 * j - 1) % count] + plane[(2 * j + 2) % count]
    )


def fine_kernel(cells, added, pair, pressure, faces, inverse, field, other, piece, packed):
    def coeff(i):
        return fine_plane(cells, added, 1, i)

    def rhs(i):
        return fine_plane(cells, added, 0, i)

    operator = Operator(22, faces)

    def begin(i, value):
        inverse[i] = value
        field[i] = omega_first * rhs(i) * value

    operator.build(coeff, begin)

    def store(i, value):
        other[i] = value
        if i < 10:
            pressure[i] = value
        elif i >= 20:
            pressure[i - 10] = value

    sweep(operator, field, inverse, rhs, omega_second, store)

    def leave(i, applied):
        field[i] = jnp.where(coeff(i) > 0, rhs(i) - applied, 0.0)

    operator.apply(other, leave)
    for j in range(11):
        planes = (restrict_planes(field, j, 22), coeff(2 * j) + coeff(2 * j + 1))
        for kind in range(2):
            for half in range(2):
                slot = piece.at[(2 * j + kind) * 2 + half]
                slot[...] = planes[kind][:, 128 * half : 128 * half + 128]
                packed[kind, pl.ds(24 * j, 24), pl.ds(128 * half, 128)] = halve_rows(slot, kind == 0)
    matrices = (
        lane_map(256, 128, lambda f, c: 4.0 * gather_weights(fine_lane(f), middle_lane(c))),
        lane_map(256, 128, lambda f, c: 0.25 * mean_weights(fine_lane(f), middle_lane(c))),
    )
    for kind in range(2):
        result = product(packed[kind], matrices[kind])
        for j in range(11):
            pair[kind, j] = result[24 * j : 24 * j + 24]


def box_kernel(pair, box, parity, corrected, faces, inverse, field, other, piece, packed, low, low_faces, low_inverse, risen):
    def coeff(i):
        return pair[1, i]

    def rhs(i):
        return pair[0, i]

    operator = Operator(16, faces)

    def begin(i, value):
        inverse[i] = value
        field[i] = omega_first * rhs(i) * value

    operator.build(coeff, begin)

    def store(i, value):
        other[i] = value

    sweep(operator, field, inverse, rhs, omega_second, store)

    def leave(i, applied):
        field[i] = jnp.where(coeff(i) > 0, rhs(i) - applied, 0.0)

    operator.apply(other, leave)
    for j in range(8):
        planes = (restrict_planes(field, j, 16), coeff(2 * j) + coeff(2 * j + 1))
        for kind in range(2):
            slot = piece.at[2 * j + kind]
            slot[...] = planes[kind]
            packed[kind, pl.ds(16 * j, 16), :] = halve_rows(slot, kind == 0)
    odd = parity[0]
    matrices = (
        lane_map(128, 128, lambda m, c: 4.0 * gather_weights(middle_lane(m), coarse_lane(c, odd))),
        lane_map(128, 128, lambda m, c: 0.25 * mean_weights(middle_lane(m), coarse_lane(c, odd))),
    )
    for kind in range(2):
        result = product(packed[kind], matrices[kind])
        for j in range(8):
            low[kind, j] = result[16 * j : 16 * j + 16] * box[j]

    coarse = Operator(8, low_faces)

    def begin_low(i, value):
        low_inverse[i] = value
        low[2, i] = omega_first * low[0, i] * value

    coarse.build(lambda i: low[1, i], begin_low)

    def store_low(i, value):
        packed[0, pl.ds(16 * i, 16), :] = value

    sweep(coarse, low.at[2], low_inverse, lambda i: low[0, i], omega_second, store_low)

    def spread_box(c, m):
        coarse, fine = coarse_lane(c, odd), middle_lane(m)
        return jnp.where(same_box(coarse, fine, odd), spread_weights(coarse, fine), 0.0)

    result = product(packed[0], lane_map(128, 128, spread_box))
    for j in range(8):
        spread_rows(result[16 * j : 16 * j + 16], risen.at[j])
    for place in range(12):
        i = place if place < 8 else place + 4
        near = (i // 2 + (1 if i % 2 else -1)) % 8
        corrected[place] = other[i] + (0.75 * risen[i // 2] + 0.25 * risen[near])


def spread_rows(values, target):
    count = values.shape[0]
    target[pl.ds(0, count, 2), :] = 0.75 * values + 0.25 * turn(values, 0, -1)
    target[pl.ds(1, count, 2), :] = 0.75 * values + 0.25 * turn(values, 0, 1)


def last_kernel(middle, pair, cells, added, pre, out, faces, inverse, field, faces_m, inverse_m, field_m, packed, risen):
    def coeff_m(i):
        return pair[1, i if i < 8 else i + 4]

    def rhs_m(i):
        return pair[0, i if i < 8 else i + 4]

    operator = Operator(12, faces_m)

    def keep_m(i, value):
        inverse_m[i] = value

    operator.build(coeff_m, keep_m)

    def store_m(i, value):
        field_m[i] = value

    sweep(operator, middle, inverse_m, rhs_m, omega_first, store_m)

    def store_packed(i, value):
        place = (i + 2) % 12
        if place < 8:
            packed[pl.ds(32 * place, 32), :] = value

    sweep(operator, field_m, inverse_m, rhs_m, omega_second, store_packed)

    def coeff(i):
        return fine_plane(cells, added, 1, i if i < 10 else i + 10)

    def rhs(i):
        return fine_plane(cells, added, 0, i if i < 10 else i + 10)

    fine = Operator(12, faces)

    def keep(i, value):
        inverse[i] = value

    fine.build(coeff, keep)
    result = product(
        packed[...], lane_map(128, 256, lambda c, f: spread_weights(middle_lane(c), fine_lane(f)))
    )
    for place in range(8):
        for half in range(2):
            spread_rows(
                result[32 * place : 32 * place + 32, 128 * half : 128 * half + 128],
                risen.at[2 * place + half],
            )

    def lifted(place):
        halves = [
            jnp.concatenate([risen[2 * place + half, 0:40], risen[2 * place + half, 56:64]], axis=0)
            for half in range(2)
        ]
        return jnp.concatenate(halves, axis=1)

    for i in range(12):
        fine_index = i if i < 10 else i - 12
        place = fine_index // 2 + 2
        near = place + (1 if fine_index % 2 else -1)
        value = 0.75 * lifted(place) + 0.25 * lifted(near)
        field[0, i] = pre[i] + jnp.where(coeff(i) > 0, value, 0.0)

    def store(i, value):
        field[1, i] = value

    sweep(fine, field.at[0], inverse, rhs, omega_first, store)

    def store_out(i, value):
        if i < 8:
            out[i] = value[:32, :128]

    sweep(fine, field.at[1], inverse, rhs, omega_second, store_out)


interpret = False
VMEM = pl.BlockSpec(memory_space=pltpu.VMEM)
SMEM = pl.BlockSpec(memory_space=pltpu.SMEM)


def call(kernel, outs, scratch, *arguments):
    return pl.pallas_call(
        kernel,
        out_shape=[jax.ShapeDtypeStruct(shape, jnp.float32) for shape in outs],
        in_specs=[VMEM if value.ndim > 1 else SMEM for value in arguments],
        out_specs=[VMEM] * len(outs),
        scratch_shapes=[pltpu.VMEM(shape, jnp.float32) for shape in scratch],
        compiler_params=pltpu.CompilerParams(vmem_limit_bytes=24 * 1024 * 1024),
        interpret=interpret,
    )(*arguments)


def take_lanes(values, matrix):
    rows = values.reshape(-1, values.shape[-1])
    return lax.dot_general(matrix, rows, (((0,), (1,)), ((), ())), precision=HIGHEST)


def put_lanes(strip, matrix, shape):
    rows = lax.dot_general(strip, matrix, (((0,), (0,)), ((), ())), precision=HIGHEST)
    return rows.reshape(shape)


def local(source, conductivity):
    low_x = lax.axis_index("gx") % 2 == 0
    low_y = lax.axis_index("gy") % 2 == 0
    odd_z = (lax.axis_index("gz") % 2).reshape(1)

    def side(low, when_low, when_high):
        return jnp.where(low, when_low, when_high)

    cells = jnp.stack([source, conductivity])
    near = swap(side(low_y, cells[:, :, 28:], cells[:, :, :4]), "gy", False)
    far = swap(side(low_y, cells[:, :, :12], cells[:, :, 20:]), "gy", True)
    cells = join([cells, side(low_y, join([near, far], 2), join([far, near], 2))], 2)

    near = swap(side(low_x, cells[:, 4:], cells[:, :4]), "gx", False)
    far = swap(side(low_x, join([cells, near[:, :2]], 1), join([near[:, 2:], cells], 1)), "gx", True)
    cells = join([cells, side(low_x, join([near, far], 1), join([far, near], 1))], 1)

    strips = take_lanes(cells, lane_map(128, 64, lambda z, k: z == k + jnp.where(k < 32, 0, 64)))
    count = lax.axis_size("gz")
    after = lax.ppermute(strips[:32], "gz", [(i + 1, i) for i in range(count - 1)])
    before = lax.ppermute(strips[32:], "gz", [(i, i + 1) for i in range(count - 1)])
    added = put_lanes(
        join([after, before], 0),
        lane_map(64, 128, lambda k, z: z == k + jnp.where(k < 32, 0, 64)),
        (2, 22, 48, 128),
    )

    plane = (48, 256)
    pair, pre_pressure = call(
        fine_kernel,
        [(2, 11, 24, 128), (12, *plane)],
        [(3, 22, *plane), (22, *plane), (22, *plane), (22, *plane), (44, 48, 128), (2, 264, 256)],
        cells,
        added,
    )

    near = swap(side(low_y, pair[:, :, 4:16], pair[:, :, :12]), "gy", False)
    pair = side(
        low_y,
        join([pair[:, :, :16], near, pair[:, :, 20:]], 2),
        join([pair[:, :, :20], near], 2),
    )
    near = swap(side(low_x, join([pair[:, 7:], pair[:, :4]], 1), pair[:, :8]), "gx", False)
    pair = side(low_x, join([pair[:, :4], near, pair[:, 7:]], 1), join([pair[:, :8], near], 1))

    place = [lax.broadcasted_iota(jnp.int32, (8, 16, 128), dim) for dim in range(3)]
    in_box = (
        side(low_x, place[0] < 4, (place[0] < 2) | (place[0] >= 6))
        & side(low_y, place[1] < 14, (place[1] < 8) | (place[1] >= 10))
    )
    (middle,) = call(
        box_kernel,
        [(12, 32, 128)],
        [(3, 16, 32, 128), (16, 32, 128), (16, 32, 128), (16, 32, 128), (16, 32, 128), (2, 128, 128)]
        + [(3, 8, 16, 128), (3, 8, 16, 128), (8, 16, 128), (8, 32, 128)],
        pair,
        in_box.astype(jnp.float32),
        odd_z,
    )

    far = swap(side(low_y, middle[:, :4], middle[:, 12:16]), "gy", True)
    middle = side(
        low_y, join([middle[:, :28], far], 1), join([middle[:, :16], far, middle[:, 20:]], 1)
    )
    far = swap(side(low_x, middle[:4], middle[:4]), "gx", True)
    middle = side(low_x, join([middle[:8], far], 0), join([middle[:4], far, middle[8:]], 0))

    (pressure,) = call(
        last_kernel,
        [(8, 32, 128)],
        [(3, 12, *plane), (12, *plane), (2, 12, *plane), (3, 12, 32, 128), (12, 32, 128), (12, 32, 128)]
        + [(256, 128), (16, 64, 128)],
        middle,
        pair,
        cells,
        added,
        pre_pressure,
    )
    return pressure


def solution(mesh):
    spec = P("gx", "gy", "gz")
    return jax.shard_map(local, mesh=mesh, in_specs=(spec, spec), out_specs=spec, check_vma=False)
```

```python
import math

import jax
import jax.numpy as jnp
from jax import lax
from jax.experimental import pallas as pl
from jax.experimental.pallas import tpu as pltpu
from jax.sharding import PartitionSpec as P

spectrum_top = 1.9
spectrum_low = 0.475
mean_value = (spectrum_top + spectrum_low) / 2
half_range = (spectrum_top - spectrum_low) / 2
omega_first = 1.0 / (mean_value + half_range * math.cos(math.pi / 4))
omega_second = 1.0 / (mean_value + half_range * math.cos(3 * math.pi / 4))
HIGHEST = lax.Precision.HIGHEST


def swap(block, axis, outer):
    count = lax.axis_size(axis)
    route = []
    for low in range(1 if outer else 0, count - 1, 2):
        route += [(low, low + 1), (low + 1, low)]
    return lax.ppermute(block, axis, route)


def cut(values, start, stop, dim):
    return lax.slice_in_dim(values, start, stop, axis=dim)


def join(pieces, dim):
    return jnp.concatenate(pieces, axis=dim)


def turn(plane, dim, step):
    return pltpu.roll(plane, -step % plane.shape[dim], dim)


class Operator:
    def __init__(self, faces, planes):
        self.faces = faces
        self.planes = list(planes)

    def build(self, coeff, take):
        count = len(self.planes)
        before = coeff(count - 1) + coeff(0)
        for i in range(count):
            here = coeff(i)
            across = here + coeff((i + 1) % count)
            rows = here + turn(here, 0, 1)
            lanes = here + turn(here, 1, 1)
            for place, face in enumerate((across, rows, lanes)):
                self.faces[place, i] = face
            diagonal = (across + before) + (rows + turn(rows, 0, -1)) + (lanes + turn(lanes, 1, -1))
            take(i, jnp.where(here > 0, 1.0 / diagonal, 0.0))
            before = across

    def apply(self, field, take):
        count = len(self.planes)
        before = self.faces[0, self.planes[-1]] * (field(count - 1) - field(0))
        for i, place in enumerate(self.planes):
            here = field(i)
            across = self.faces[0, place] * (here - field((i + 1) % count))
            rows = self.faces[1, place] * (here - turn(here, 0, 1))
            lanes = self.faces[2, place] * (here - turn(here, 1, 1))
            take(i, (across - before) + (rows - turn(rows, 0, -1)) + (lanes - turn(lanes, 1, -1)))
            before = across


def sweep(operator, field, inverse, rhs, omega, store):
    def take(i, applied):
        store(i, field(i) + (omega * (rhs(i) - applied)) * inverse(i))

    operator.apply(field, take)


def plane_of(ref, *lead):
    return lambda i: ref[(*lead, i)]


def keep_in(ref, *lead):
    def store(i, value):
        ref[(*lead, i)] = value

    return store


def halve_rows(piece, weights):
    count = piece.shape[0] // 2
    even = piece[pl.ds(0, count, 2), :]
    odd = piece[pl.ds(1, count, 2), :]
    if not weights:
        return even + odd
    return 0.375 * (even + odd) + 0.125 * (turn(odd, 0, -1) + turn(even, 0, 1))


def product(values, matrix):
    return jnp.dot(values, matrix, precision=HIGHEST, preferred_element_type=jnp.float32)


def lane_map(rows, columns, entries):
    row = lax.broadcasted_iota(jnp.int32, (rows, columns), 0)
    column = lax.broadcasted_iota(jnp.int32, (rows, columns), 1)
    return entries(row, column).astype(jnp.float32)


def signed(index, size, after):
    return jnp.where(index < after, index, index - size)


def gather_weights(fine, coarse):
    step = fine - 2 * coarse
    return jnp.where((step == 0) | (step == 1), 0.375, jnp.where((step == -1) | (step == 2), 0.125, 0.0))


def mean_weights(fine, coarse):
    step = fine - 2 * coarse
    return jnp.where((step == 0) | (step == 1), 0.5, 0.0)


def spread_weights(coarse, fine):
    step = fine - 2 * coarse
    return jnp.where((step == 0) | (step == 1), 0.75, jnp.where((step == -1) | (step == 2), 0.25, 0.0))


def fine_lane(f):
    return signed(f, 256, 192)


def middle_lane(m):
    return signed(m, 128, 96)


def coarse_lane(lane, odd):
    after = jnp.where(lane < 32, lane, jnp.where((lane == 32) & (odd == 1), 4096, lane - odd))
    before = jnp.where((lane == 127) & (odd == 0), 4096, lane - 127 - odd)
    return jnp.where(lane < 64, after, before)


def same_box(coarse, middle, odd):
    edge = 32 * odd
    return (coarse >= edge) == (middle >= 2 * edge)


def restrict_planes(plane, j, count):
    return 0.375 * (plane(2 * j) + plane(2 * j + 1)) + 0.125 * (
        plane((2 * j - 1) % count) + plane((2 * j + 2) % count)
    )


def restrict_level(plane, coeff, count, piece, packed, matrices, store):
    rows, lanes = piece.shape[1:]
    halves = plane(0).shape[1] // lanes
    for j in range(count // 2):
        planes = (restrict_planes(plane, j, count), coeff(2 * j) + coeff(2 * j + 1))
        for kind in range(2):
            for half in range(halves):
                slot = piece.at[(2 * j + kind) * halves + half]
                slot[...] = planes[kind][:, lanes * half : lanes * half + lanes]
                packed[kind, pl.ds(rows // 2 * j, rows // 2), pl.ds(lanes * half, lanes)] = halve_rows(
                    slot, kind == 0
                )
    for kind in range(2):
        result = product(packed[kind], matrices[kind])
        for j in range(count // 2):
            store(kind, j, result[rows // 2 * j : rows // 2 * (j + 1)])


fine_places = [*range(10), 20, 21]
middle_places = [*range(8), *range(12, 16)]


def fine_kernel(wide, pair, kept, faces, inverse, rhs, pre, coeff, field, piece, packed):
    lane = lax.broadcasted_iota(jnp.int32, (48, 128), 1)
    edge = (lane < 32) | (lane >= 96)
    for i in range(22):
        halo = wide[2, i]
        rhs[i, :, 0:128] = 2.0 * wide[0, i]
        rhs[i, :, 128:256] = jnp.where(edge, 2.0 * halo, 0.0)
        coeff[i, :, 0:128] = wide[1, i]
        coeff[i, :, 128:256] = jnp.where(edge, pltpu.roll(halo, 64, 1), 0.0)
    operator = Operator(faces, range(22))

    def begin(i, value):
        inverse[i] = value
        field[i] = omega_first * rhs[i] * value

    operator.build(plane_of(coeff), begin)
    sweep(operator, plane_of(field), plane_of(inverse), plane_of(rhs), omega_second, keep_in(pre))

    def leave(i, applied):
        field[i] = jnp.where(coeff[i] > 0, rhs[i] - applied, 0.0)

    operator.apply(plane_of(pre), leave)
    matrices = (
        lane_map(256, 128, lambda f, c: 4.0 * gather_weights(fine_lane(f), middle_lane(c))),
        lane_map(256, 128, lambda f, c: 0.25 * mean_weights(fine_lane(f), middle_lane(c))),
    )

    def store(kind, j, value):
        pair[kind, j] = value

    restrict_level(plane_of(field), plane_of(coeff), 22, piece, packed, matrices, store)
    for i, place in enumerate(fine_places):
        for kind, values in enumerate((coeff, rhs, pre)):
            kept[kind, i] = values[place]


def box_kernel(pair, box, parity, corrected, kept, faces, inverse, field, other, piece, packed, low, low_faces, low_inverse, risen):
    rhs, coeff = plane_of(pair, 0), plane_of(pair, 1)
    operator = Operator(faces, range(16))

    def begin(i, value):
        inverse[i] = value
        field[i] = omega_first * rhs(i) * value

    operator.build(coeff, begin)
    sweep(operator, plane_of(field), plane_of(inverse), rhs, omega_second, keep_in(other))

    def leave(i, applied):
        field[i] = jnp.where(coeff(i) > 0, rhs(i) - applied, 0.0)

    operator.apply(plane_of(other), leave)
    odd = parity[0]
    matrices = (
        lane_map(128, 128, lambda m, c: 4.0 * gather_weights(middle_lane(m), coarse_lane(c, odd))),
        lane_map(128, 128, lambda m, c: 0.25 * mean_weights(middle_lane(m), coarse_lane(c, odd))),
    )

    def store(kind, j, value):
        low[kind, j] = value * box[j]

    restrict_level(plane_of(field), coeff, 16, piece, packed, matrices, store)
    coarse = Operator(low_faces, range(8))

    def begin_low(i, value):
        low_inverse[i] = value
        low[2, i] = omega_first * low[0, i] * value

    coarse.build(plane_of(low, 1), begin_low)

    def store_low(i, value):
        packed[0, pl.ds(16 * i, 16), :] = value

    sweep(coarse, plane_of(low, 2), plane_of(low_inverse), plane_of(low, 0), omega_second, store_low)

    def spread_box(c, m):
        coarse, fine = coarse_lane(c, odd), middle_lane(m)
        return jnp.where(same_box(coarse, fine, odd), spread_weights(coarse, fine), 0.0)

    result = product(packed[0], lane_map(128, 128, spread_box))
    for j in range(8):
        spread_rows(result[16 * j : 16 * j + 16], risen.at[j])
    for place, i in enumerate(middle_places):
        for kind, values in enumerate((faces.at[0], faces.at[1], faces.at[2], inverse, pair.at[0])):
            kept[kind, place] = values[i]
        near = (i // 2 + (1 if i % 2 else -1)) % 8
        corrected[place] = other[i] + (0.75 * risen[i // 2] + 0.25 * risen[near])


def spread_rows(values, target):
    count = values.shape[0]
    target[pl.ds(0, count, 2), :] = 0.75 * values + 0.25 * turn(values, 0, -1)
    target[pl.ds(1, count, 2), :] = 0.75 * values + 0.25 * turn(values, 0, 1)


def last_kernel(middle, kept_m, kept, out, faces, inverse, field, field_m, packed, risen):
    operator = Operator(kept_m, range(12))
    inverse_m, rhs_m = plane_of(kept_m, 3), plane_of(kept_m, 4)
    sweep(operator, plane_of(middle), inverse_m, rhs_m, omega_first, keep_in(field_m))

    def store_packed(i, value):
        place = (i + 2) % 12
        if place < 8:
            packed[pl.ds(32 * place, 32), :] = value

    sweep(operator, plane_of(field_m), inverse_m, rhs_m, omega_second, store_packed)
    result = product(
        packed[...], lane_map(128, 256, lambda c, f: spread_weights(middle_lane(c), fine_lane(f)))
    )
    for place in range(8):
        for half in range(2):
            spread_rows(
                result[32 * place : 32 * place + 32, 128 * half : 128 * half + 128],
                risen.at[2 * place + half],
            )

    def lifted(place):
        halves = [
            jnp.concatenate([risen[2 * place + half, 0:40], risen[2 * place + half, 56:64]], axis=0)
            for half in range(2)
        ]
        return jnp.concatenate(halves, axis=1)

    fine = Operator(faces, range(12))
    fine.build(plane_of(kept, 0), keep_in(inverse))
    for i in range(12):
        fine_index = i if i < 10 else i - 12
        place = fine_index // 2 + 2
        near = place + (1 if fine_index % 2 else -1)
        value = 0.75 * lifted(place) + 0.25 * lifted(near)
        field[0, i] = kept[2, i] + jnp.where(kept[0, i] > 0, value, 0.0)

    rhs_f, inverse_f = plane_of(kept, 1), plane_of(inverse)
    sweep(fine, plane_of(field, 0), inverse_f, rhs_f, omega_first, keep_in(field, 1))

    def store_out(i, value):
        if i < 8:
            out[i] = value[:32, :128]

    sweep(fine, plane_of(field, 1), inverse_f, rhs_f, omega_second, store_out)


interpret = False
VMEM = pl.BlockSpec(memory_space=pltpu.VMEM)
SMEM = pl.BlockSpec(memory_space=pltpu.SMEM)


def call(kernel, outs, scratch, *arguments):
    return pl.pallas_call(
        kernel,
        out_shape=[jax.ShapeDtypeStruct(shape, jnp.float32) for shape in outs],
        in_specs=[VMEM if value.ndim > 1 else SMEM for value in arguments],
        out_specs=[VMEM] * len(outs),
        scratch_shapes=[pltpu.VMEM(shape, jnp.float32) for shape in scratch],
        compiler_params=pltpu.CompilerParams(vmem_limit_bytes=24 * 1024 * 1024),
        interpret=interpret,
    )(*arguments)


def take_lanes(values, matrix):
    rows = values.reshape(-1, values.shape[-1])
    return lax.dot_general(matrix, rows, (((0,), (1,)), ((), ())), precision=HIGHEST)


def put_lanes(strip, matrix, shape):
    rows = lax.dot_general(strip, matrix, (((0,), (0,)), ((), ())), precision=HIGHEST)
    return rows.reshape(shape)


def local(source, conductivity):
    low_x = lax.axis_index("gx") % 2 == 0
    low_y = lax.axis_index("gy") % 2 == 0
    odd_z = (lax.axis_index("gz") % 2).reshape(1)

    def side(low, when_low, when_high):
        return jnp.where(low, when_low, when_high)

    cells = jnp.stack([source, conductivity])
    sent = lax.optimization_barrier(
        side(
            low_y,
            join([cells[:, :, :12], cells[:, :, 28:]], 2),
            join([cells[:, :, 20:], cells[:, :, :4]], 2),
        )
    )
    far = swap(sent[:, :, :12], "gy", True)
    near = swap(sent[:, :, 12:], "gy", False)
    cells = join([cells, side(low_y, join([near, far], 2), join([far, near], 2))], 2)

    strips = take_lanes(cells, lane_map(128, 64, lambda z, k: z == k + jnp.where(k < 32, 0, 64)))
    count = lax.axis_size("gz")
    after = lax.ppermute(strips[:32], "gz", [(i + 1, i) for i in range(count - 1)])
    before = lax.ppermute(strips[32:], "gz", [(i, i + 1) for i in range(count - 1)])
    rows = strips.shape[1] // 2
    halo = join([after[:, :rows], before[:, rows:], after[:, rows:], before[:, :rows]], 0)
    halo = put_lanes(halo, lane_map(128, 128, lambda k, z: k == z), (1, 8, 48, 128))
    cells = join([cells, halo], 0)

    far = swap(cells, "gx", True)
    near = swap(side(low_x, cells[:, 4:], cells[:, :4]), "gx", False)
    last = swap(side(low_x, near[:, :2], near[:, 2:]), "gx", True)
    wide = join([cells, side(low_x, join([near, last, far], 1), join([far, last, near], 1))], 1)

    plane = (48, 256)
    pair, kept = call(
        fine_kernel,
        [(2, 11, 24, 128), (3, 12, *plane)],
        [(3, 22, *plane)] + [(22, *plane)] * 5 + [(44, 48, 128), (2, 264, 256)],
        wide,
    )

    pair = side(low_x, join([pair[:, 7:], pair[:, :4]], 1), pair[:, :8])
    near = swap(side(low_y, pair[:, :, 4:16], pair[:, :, :12]), "gy", False)
    pair = side(
        low_y,
        join([pair[:, :, :16], near, pair[:, :, 20:]], 2),
        join([pair[:, :, :20], near], 2),
    )
    near = swap(pair, "gx", False)
    pair = side(low_x, join([pair[:, 4:], near, pair[:, :4]], 1), join([pair, near], 1))

    place = [lax.broadcasted_iota(jnp.int32, (8, 16, 128), dim) for dim in range(3)]
    in_box = (
        side(low_x, place[0] < 4, (place[0] < 2) | (place[0] >= 6))
        & side(low_y, place[1] < 14, (place[1] < 8) | (place[1] >= 10))
    )
    middle, kept_m = call(
        box_kernel,
        [(12, 32, 128), (5, 12, 32, 128)],
        [(3, 16, 32, 128), (16, 32, 128), (16, 32, 128), (16, 32, 128), (16, 32, 128), (2, 128, 128)]
        + [(3, 8, 16, 128), (3, 8, 16, 128), (8, 16, 128), (8, 32, 128)],
        pair,
        in_box.astype(jnp.float32),
        odd_z,
    )

    far = swap(side(low_y, middle[:, :4], middle[:, 12:16]), "gy", True)
    middle = side(
        low_y, join([middle[:, :28], far], 1), join([middle[:, :16], far, middle[:, 20:]], 1)
    )
    far = swap(side(low_x, middle[:4], middle[:4]), "gx", True)
    middle = side(low_x, join([middle[:8], far], 0), join([middle[:4], far, middle[8:]], 0))

    (pressure,) = call(
        last_kernel,
        [(8, 32, 128)],
        [(3, 12, *plane), (12, *plane), (2, 12, *plane), (12, 32, 128), (256, 128), (16, 64, 128)],
        middle,
        kept_m,
        kept,
    )
    return pressure


def solution(mesh):
    spec = P("gx", "gy", "gz")
    return jax.shard_map(local, mesh=mesh, in_specs=(spec, spec), out_specs=spec, check_vma=False)
```

```python
import math

import jax
import jax.numpy as jnp
from jax import lax
from jax.experimental import pallas as pl
from jax.experimental.pallas import tpu as pltpu
from jax.sharding import PartitionSpec as P

spectrum_top = 1.9
spectrum_low = 0.475
mean_value = (spectrum_top + spectrum_low) / 2
half_range = (spectrum_top - spectrum_low) / 2
omega_first = 1.0 / (mean_value + half_range * math.cos(math.pi / 4))
omega_second = 1.0 / (mean_value + half_range * math.cos(3 * math.pi / 4))
HIGHEST = lax.Precision.HIGHEST


def swap(block, axis, outer):
    count = lax.axis_size(axis)
    route = []
    for low in range(1 if outer else 0, count - 1, 2):
        route += [(low, low + 1), (low + 1, low)]
    return lax.ppermute(block, axis, route)


def cut(values, start, stop, dim):
    return lax.slice_in_dim(values, start, stop, axis=dim)


def join(pieces, dim):
    return jnp.concatenate(pieces, axis=dim)


def turn(plane, dim, step):
    return pltpu.roll(plane, -step % plane.shape[dim], dim)


class Operator:
    def __init__(self, faces):
        self.faces = faces

    def build(self, coeff, start, stop, take):
        before = coeff(start - 1) + coeff(start)
        self.faces[0, start - 1] = before
        for i in range(start, stop):
            here = coeff(i)
            across = here + coeff(i + 1)
            rows = here + turn(here, 0, 1)
            lanes = here + turn(here, 1, 1)
            for place, face in enumerate((across, rows, lanes)):
                self.faces[place, i] = face
            diagonal = (across + before) + (rows + turn(rows, 0, -1)) + (lanes + turn(lanes, 1, -1))
            take(i, jnp.where(here > 0, 1.0 / diagonal, 0.0))
            before = across

    def apply(self, field, start, stop, take):
        before = self.faces[0, start - 1] * (field(start - 1) - field(start))
        for i in range(start, stop):
            here = field(i)
            across = self.faces[0, i] * (here - field(i + 1))
            rows = self.faces[1, i] * (here - turn(here, 0, 1))
            lanes = self.faces[2, i] * (here - turn(here, 1, 1))
            take(i, (across - before) + (rows - turn(rows, 0, -1)) + (lanes - turn(lanes, 1, -1)))
            before = across


def sweep(operator, field, inverse, rhs, omega, start, stop, store):
    def take(i, applied):
        store(i, field(i) + (omega * (rhs(i) - applied)) * inverse(i))

    operator.apply(field, start, stop, take)


def plane_of(ref, *lead):
    return lambda i: ref[(*lead, i)]


def keep_in(ref, *lead):
    def store(i, value):
        ref[(*lead, i)] = value

    return store


def halve_rows(piece, weights):
    count = piece.shape[0] // 2
    even = piece[pl.ds(0, count, 2), :]
    odd = piece[pl.ds(1, count, 2), :]
    if not weights:
        return even + odd
    return 0.375 * (even + odd) + 0.125 * (turn(odd, 0, -1) + turn(even, 0, 1))


def product(values, matrix):
    return jnp.dot(values, matrix, precision=HIGHEST, preferred_element_type=jnp.float32)


def lane_map(rows, columns, entries):
    row = lax.broadcasted_iota(jnp.int32, (rows, columns), 0)
    column = lax.broadcasted_iota(jnp.int32, (rows, columns), 1)
    return entries(row, column).astype(jnp.float32)


def signed(index, size, after):
    return jnp.where(index < after, index, index - size)


def gather_weights(fine, coarse):
    step = fine - 2 * coarse
    return jnp.where((step == 0) | (step == 1), 0.375, jnp.where((step == -1) | (step == 2), 0.125, 0.0))


def mean_weights(fine, coarse):
    step = fine - 2 * coarse
    return jnp.where((step == 0) | (step == 1), 0.5, 0.0)


def spread_weights(coarse, fine):
    step = fine - 2 * coarse
    return jnp.where((step == 0) | (step == 1), 0.75, jnp.where((step == -1) | (step == 2), 0.25, 0.0))


def fine_lane(f):
    return signed(f, 256, 192)


def middle_lane(m):
    return signed(m, 128, 96)


def coarse_lane(lane, odd):
    after = jnp.where(lane < 32, lane, jnp.where((lane == 32) & (odd == 1), 4096, lane - odd))
    before = jnp.where((lane == 127) & (odd == 0), 4096, lane - 127 - odd)
    return jnp.where(lane < 64, after, before)


def same_box(coarse, middle, odd):
    edge = 32 * odd
    return (coarse >= edge) == (middle >= 2 * edge)


def restrict_level(plane, coeff, first, count, piece, packed, matrices, store):
    rows, lanes = piece.shape[1:]
    parts = packed.shape[2] // lanes
    for j in range(count):
        at = first + 2 * j
        planes = (
            0.375 * (plane(at) + plane(at + 1)) + 0.125 * (plane(at - 1) + plane(at + 2)),
            coeff(at) + coeff(at + 1),
        )
        for kind in range(2):
            for part in range(parts):
                slot = piece.at[(2 * j + kind) * parts + part]
                slot[...] = planes[kind][:, lanes * part : lanes * part + lanes]
                packed[kind, pl.ds(rows // 2 * j, rows // 2), pl.ds(lanes * part, lanes)] = halve_rows(
                    slot, kind == 0
                )
    for kind in range(2):
        result = product(packed[kind], matrices[kind])
        for j in range(count):
            store(kind, j, result[rows // 2 * j : rows // 2 * (j + 1)])


def first_kernel(source, conductivity, parity, far, near):
    for kind, values in enumerate((source, conductivity)):
        for odd in range(2):

            @pl.when(parity[0] == odd)
            def _(kind=kind, values=values, odd=odd):
                for i in range(8):
                    far[kind, i] = values[i, 20:32] if odd else values[i, 0:12]
                    near[kind, i] = values[i, 0:4] if odd else values[i, 28:32]


def fine_kernel(wide, pair, kept, faces, inverse, rhs, coeff, field, pre, piece, packed):
    lane = lax.broadcasted_iota(jnp.int32, (48, 128), 1)
    edge = (lane < 32) | (lane >= 96)
    for i in range(16):
        halo = wide[2, i]
        rhs[i, :, 0:128] = 2.0 * wide[0, i]
        rhs[i, :, 128:256] = jnp.where(edge, 2.0 * halo, 0.0)
        coeff[i, :, 0:128] = wide[1, i]
        coeff[i, :, 128:256] = jnp.where(edge, pltpu.roll(halo, 64, 1), 0.0)
    operator = Operator(faces)

    def begin(i, value):
        inverse[i] = value
        field[i] = omega_first * rhs[i] * value

    operator.build(plane_of(coeff), 1, 15, begin)

    def store_pre(i, value):
        pre[i] = value
        kept[0, i - 2] = coeff[i]
        kept[1, i - 2] = rhs[i]
        kept[2, i - 2] = value

    sweep(operator, plane_of(field), plane_of(inverse), plane_of(rhs), omega_second, 2, 14, store_pre)

    def leave(i, applied):
        field[i] = jnp.where(coeff[i] > 0, rhs[i] - applied, 0.0)

    operator.apply(plane_of(pre), 3, 13, leave)
    matrices = (
        lane_map(256, 128, lambda f, c: 4.0 * gather_weights(fine_lane(f), middle_lane(c))),
        lane_map(256, 128, lambda f, c: 0.25 * mean_weights(fine_lane(f), middle_lane(c))),
    )

    def store(kind, j, value):
        pair[kind, j] = value

    restrict_level(plane_of(field), plane_of(coeff), 4, 4, piece, packed, matrices, store)


def box_kernel(pair, box, parity, corrected, faces, inverse, field, other, piece, packed, low, low_faces, low_inverse, risen):
    rhs, coeff = plane_of(pair, 0), plane_of(pair, 1)
    operator = Operator(faces)

    def begin(i, value):
        inverse[i] = value
        field[i] = omega_first * rhs(i) * value

    operator.build(coeff, 1, 15, begin)
    sweep(operator, plane_of(field), plane_of(inverse), rhs, omega_second, 2, 14, keep_in(other))

    def leave(i, applied):
        field[i] = jnp.where(coeff(i) > 0, rhs(i) - applied, 0.0)

    operator.apply(plane_of(other), 3, 13, leave)
    odd = parity[0]
    matrices = (
        lane_map(128, 128, lambda m, c: 4.0 * gather_weights(middle_lane(m), coarse_lane(c, odd))),
        lane_map(128, 128, lambda m, c: 0.25 * mean_weights(middle_lane(m), coarse_lane(c, odd))),
    )
    in_box = box[...]

    def store(kind, j, value):
        low[kind, j + 1] = value * in_box

    restrict_level(plane_of(field), coeff, 4, 4, piece, packed, matrices, store)
    for place in (0, 5):
        for kind in range(3):
            low[kind, place] = jnp.zeros((16, 128), jnp.float32)
    coarse = Operator(low_faces)

    def begin_low(i, value):
        low_inverse[i] = value
        low[2, i] = omega_first * low[0, i] * value

    coarse.build(plane_of(low, 1), 1, 5, begin_low)

    def store_low(i, value):
        packed[0, pl.ds(16 * (i - 1), 16), :] = value

    sweep(coarse, plane_of(low, 2), plane_of(low_inverse), plane_of(low, 0), omega_second, 1, 5, store_low)

    def spread_box(c, m):
        coarse, fine = coarse_lane(c, odd), middle_lane(m)
        return jnp.where(same_box(coarse, fine, odd), spread_weights(coarse, fine), 0.0)

    result = product(packed[0], lane_map(128, 128, spread_box))
    for j in range(4):
        spread_rows(result[16 * j : 16 * j + 16], risen.at[j])
    for i in range(8):
        value = 0.75 * risen[i // 2]
        near = i // 2 + (1 if i % 2 else -1)
        if 0 <= near < 4:
            value = value + 0.25 * risen[near]
        corrected[i] = other[i + 4] + value


def spread_rows(values, target):
    count = values.shape[0]
    target[pl.ds(0, count, 2), :] = 0.75 * values + 0.25 * turn(values, 0, -1)
    target[pl.ds(1, count, 2), :] = 0.75 * values + 0.25 * turn(values, 0, 1)


def last_kernel(middle, pair, kept, out, faces, inverse, field, faces_m, inverse_m, field_m, packed, risen):
    operator = Operator(faces_m)
    rhs_m, at_m = plane_of(pair, 0), plane_of(inverse_m)
    operator.build(plane_of(pair, 1), 1, 11, keep_in(inverse_m))
    sweep(operator, plane_of(middle), at_m, rhs_m, omega_first, 1, 11, keep_in(field_m))

    def store_packed(i, value):
        packed[pl.ds(32 * (i - 2), 32), :] = value

    sweep(operator, plane_of(field_m), at_m, rhs_m, omega_second, 2, 10, store_packed)
    result = product(
        packed[...], lane_map(128, 256, lambda c, f: spread_weights(middle_lane(c), fine_lane(f)))
    )
    for place in range(8):
        for half in range(2):
            spread_rows(
                result[32 * place : 32 * place + 32, 128 * half : 128 * half + 128],
                risen.at[2 * place + half],
            )

    def lifted(place):
        halves = [
            jnp.concatenate([risen[2 * place + half, 0:40], risen[2 * place + half, 56:64]], axis=0)
            for half in range(2)
        ]
        return jnp.concatenate(halves, axis=1)

    fine = Operator(faces)
    coeff, rhs = plane_of(kept, 0), plane_of(kept, 1)
    fine.build(coeff, 1, 11, keep_in(inverse))
    for i in range(12):
        place = i // 2 + 1
        value = 0.75 * lifted(place) + 0.25 * lifted(place + (1 if i % 2 else -1))
        field[0, i] = kept[2, i] + jnp.where(coeff(i) > 0, value, 0.0)
    sweep(fine, plane_of(field, 0), plane_of(inverse), rhs, omega_first, 1, 11, keep_in(field, 1))

    def store_out(i, value):
        out[i - 2] = value[:32, :128]

    sweep(fine, plane_of(field, 1), plane_of(inverse), rhs, omega_second, 2, 10, store_out)


interpret = False
VMEM = pl.BlockSpec(memory_space=pltpu.VMEM)
SMEM = pl.BlockSpec(memory_space=pltpu.SMEM)


def call(kernel, outs, scratch, *arguments):
    return pl.pallas_call(
        kernel,
        out_shape=[jax.ShapeDtypeStruct(shape, jnp.float32) for shape in outs],
        in_specs=[VMEM if value.ndim > 1 else SMEM for value in arguments],
        out_specs=[VMEM] * len(outs),
        scratch_shapes=[pltpu.VMEM(shape, jnp.float32) for shape in scratch],
        compiler_params=pltpu.CompilerParams(vmem_limit_bytes=24 * 1024 * 1024),
        interpret=interpret,
    )(*arguments)


def take_lanes(values, matrix):
    rows = values.reshape(-1, values.shape[-1])
    return lax.dot_general(matrix, rows, (((0,), (1,)), ((), ())), precision=HIGHEST)


def put_lanes(strip, matrix, shape):
    rows = lax.dot_general(strip, matrix, (((0,), (0,)), ((), ())), precision=HIGHEST)
    return rows.reshape(shape)


def local(source, conductivity):
    low_x = lax.axis_index("gx") % 2 == 0
    low_y = lax.axis_index("gy") % 2 == 0
    odd_z = (lax.axis_index("gz") % 2).reshape(1)

    def side(low, when_low, when_high):
        return jnp.where(low, when_low, when_high)

    far, near = call(
        first_kernel,
        [(2, 8, 12, 128), (2, 8, 4, 128)],
        [],
        source,
        conductivity,
        (lax.axis_index("gy") % 2).reshape(1),
    )
    far = swap(far, "gy", True)
    near = swap(near, "gy", False)
    cells = jnp.stack([source, conductivity])
    cells = join([cells, side(low_y, join([near, far], 2), join([far, near], 2))], 2)

    strips = take_lanes(cells, lane_map(128, 64, lambda z, k: z == k + jnp.where(k < 32, 0, 64)))
    count = lax.axis_size("gz")
    after = lax.ppermute(strips[:32], "gz", [(i + 1, i) for i in range(count - 1)])
    before = lax.ppermute(strips[32:], "gz", [(i, i + 1) for i in range(count - 1)])
    rows = strips.shape[1] // 2
    halo = join([after[:, :rows], before[:, rows:], after[:, rows:], before[:, :rows]], 0)
    halo = put_lanes(halo, lane_map(128, 128, lambda k, z: k == z), (1, 8, 48, 128))
    cells = join([cells, halo], 0)

    far = swap(side(low_x, cells[:, :4], cells[:, 4:]), "gx", True)
    near = swap(side(low_x, cells[:, 4:], cells[:, :4]), "gx", False)
    wide = join([side(low_x, far, near), cells, side(low_x, near, far)], 1)

    plane = (48, 256)
    pair, kept = call(
        fine_kernel,
        [(2, 4, 24, 128), (3, 12, *plane)],
        [(3, 16, *plane)] + [(16, *plane)] * 5 + [(16, 48, 128), (2, 96, 256)],
        wide,
    )

    near = swap(side(low_y, pair[:, :, 4:16], pair[:, :, :12]), "gy", False)
    pair = side(
        low_y,
        join([pair[:, :, :16], near, pair[:, :, 20:]], 2),
        join([pair[:, :, :20], near], 2),
    )
    far = swap(pair, "gx", True)
    pair = side(low_x, join([far, pair], 1), join([pair, far], 1))
    near = swap(pair, "gx", False)
    pair = side(low_x, join([pair, near], 1), join([near, pair], 1))

    row = lax.broadcasted_iota(jnp.int32, (16, 128), 0)
    in_box = side(low_y, row < 14, (row < 8) | (row >= 10))
    (middle,) = call(
        box_kernel,
        [(8, 32, 128)],
        [(3, 16, 32, 128), (16, 32, 128), (16, 32, 128), (16, 32, 128), (8, 32, 128), (2, 64, 128)]
        + [(3, 6, 16, 128), (3, 6, 16, 128), (6, 16, 128), (4, 32, 128)],
        pair,
        in_box.astype(jnp.float32),
        odd_z,
    )

    far = swap(side(low_y, middle[:, :4], middle[:, 12:16]), "gy", True)
    middle = side(
        low_y, join([middle[:, :28], far], 1), join([middle[:, :16], far, middle[:, 20:]], 1)
    )
    far = swap(side(low_x, middle[:4], middle[4:]), "gx", True)
    middle = side(low_x, join([far, middle], 0), join([middle, far], 0))

    (pressure,) = call(
        last_kernel,
        [(8, 32, 128)],
        [(3, 12, *plane), (12, *plane), (2, 12, *plane), (3, 12, 32, 128), (12, 32, 128), (12, 32, 128)]
        + [(256, 128), (16, 64, 128)],
        middle,
        side(low_x, pair[:, :12], pair[:, 4:]),
        kept,
    )
    return pressure


def solution(mesh):
    spec = P("gx", "gy", "gz")
    return jax.shard_map(local, mesh=mesh, in_specs=(spec, spec), out_specs=spec, check_vma=False)
```

```python
import math

import jax
import jax.numpy as jnp
from jax import lax
from jax.experimental import pallas as pl
from jax.experimental.pallas import tpu as pltpu
from jax.sharding import PartitionSpec as P

spectrum_top = 1.9
spectrum_low = 0.475
mean_value = (spectrum_top + spectrum_low) / 2
half_range = (spectrum_top - spectrum_low) / 2
omega_first = 1.0 / (mean_value + half_range * math.cos(math.pi / 4))
omega_second = 1.0 / (mean_value + half_range * math.cos(3 * math.pi / 4))
HIGHEST = lax.Precision.HIGHEST


def swap(block, axis, outer):
    count = lax.axis_size(axis)
    route = []
    for low in range(1 if outer else 0, count - 1, 2):
        route += [(low, low + 1), (low + 1, low)]
    return lax.ppermute(block, axis, route)


def shift(block, axis, step):
    count = lax.axis_size(axis)
    return lax.ppermute(block, axis, [(i, i + step) for i in range(count) if 0 <= i + step < count])


def cut(values, start, stop, dim):
    return lax.slice_in_dim(values, start, stop, axis=dim)


def join(pieces, dim):
    return jnp.concatenate(pieces, axis=dim)


def turn(plane, dim, step):
    return pltpu.roll(plane, -step % plane.shape[dim], dim)


class Operator:
    def __init__(self, faces):
        self.faces = faces

    def build(self, coeff, start, stop, take):
        before = coeff(start - 1) + coeff(start)
        self.faces[0, start - 1] = before
        for i in range(start, stop):
            here = coeff(i)
            across = here + coeff(i + 1)
            rows = here + turn(here, 0, 1)
            lanes = here + turn(here, 1, 1)
            for place, face in enumerate((across, rows, lanes)):
                self.faces[place, i] = face
            if take is not None:
                diagonal = (across + before) + (rows + turn(rows, 0, -1)) + (lanes + turn(lanes, 1, -1))
                take(i, jnp.where(here > 0, 1.0 / diagonal, 0.0))
            before = across

    def apply(self, field, start, stop, take):
        before = self.faces[0, start - 1] * (field(start - 1) - field(start))
        for i in range(start, stop):
            here = field(i)
            across = self.faces[0, i] * (here - field(i + 1))
            rows = self.faces[1, i] * (here - turn(here, 0, 1))
            lanes = self.faces[2, i] * (here - turn(here, 1, 1))
            take(i, (across - before) + (rows - turn(rows, 0, -1)) + (lanes - turn(lanes, 1, -1)))
            before = across


def sweep(operator, field, inverse, rhs, omega, start, stop, store):
    def take(i, applied):
        store(i, field(i) + (omega * (rhs(i) - applied)) * inverse(i))

    operator.apply(field, start, stop, take)


class BoxOperator:
    def __init__(self, upper, lower, faces):
        self.upper = upper
        self.lower = lower
        self.faces = faces

    def build(self, coeff, start, stop, take):
        before = coeff(start - 1) + coeff(start)
        self.faces[0, start - 1] = before
        for i in range(start, stop):
            here = coeff(i)
            across = here + coeff(i + 1)
            rows = here + self.upper * turn(here, 0, 1)
            back = here + self.lower * turn(here, 0, -1)
            lanes = here + turn(here, 1, 1)
            for place, face in enumerate((across, rows, lanes, back)):
                self.faces[place, i] = face
            diagonal = (across + before) + (rows + back) + (lanes + turn(lanes, 1, -1))
            take(i, jnp.where(here > 0, 1.0 / diagonal, 0.0))
            before = across

    def apply(self, field, start, stop, take):
        before = self.faces[0, start - 1] * (field(start - 1) - field(start))
        for i in range(start, stop):
            here = field(i)
            across = self.faces[0, i] * (here - field(i + 1))
            rows = self.faces[1, i] * (here - self.upper * turn(here, 0, 1))
            back = self.faces[3, i] * (here - self.lower * turn(here, 0, -1))
            lanes = self.faces[2, i] * (here - turn(here, 1, 1))
            take(i, (across - before) + (rows + back) + (lanes - turn(lanes, 1, -1)))
            before = across


def plane_of(ref, *lead):
    return lambda i: ref[(*lead, i)]


def keep_in(ref, *lead):
    def store(i, value):
        ref[(*lead, i)] = value

    return store


def halve_circular(plane, slot, weights):
    count = plane.shape[0] // 2
    slot[...] = plane
    even = slot[pl.ds(0, count, 2), :]
    odd = slot[pl.ds(1, count, 2), :]
    if not weights:
        return even + odd
    return 0.375 * (even + odd) + 0.125 * (turn(odd, 0, -1) + turn(even, 0, 1))


def halve_own(plane, slot, weights):
    slot[0:8] = plane[32:40]
    slot[8:40] = plane[0:32]
    slot[40:48] = plane[32:40]
    even = slot[pl.ds(8, 16, 2), :]
    odd = slot[pl.ds(9, 16, 2), :]
    if not weights:
        return even + odd
    return 0.375 * (even + odd) + 0.125 * (slot[pl.ds(7, 16, 2), :] + slot[pl.ds(10, 16, 2), :])


def near_rows(plane, own):
    row = lax.broadcasted_iota(jnp.int32, (8, plane.shape[1]), 0)
    edge = jnp.where(row < 4, plane[own : own + 8], plane[plane.shape[0] - 8 :])
    return jnp.concatenate([plane[:own], edge], axis=0)


def product(values, matrix):
    return jnp.dot(values, matrix, precision=HIGHEST, preferred_element_type=jnp.float32)


def lane_map(rows, columns, entries):
    row = lax.broadcasted_iota(jnp.int32, (rows, columns), 0)
    column = lax.broadcasted_iota(jnp.int32, (rows, columns), 1)
    return entries(row, column).astype(jnp.float32)


def signed(index, size, after):
    return jnp.where(index < after, index, index - size)


def gather_weights(fine, coarse):
    step = fine - 2 * coarse
    return jnp.where((step == 0) | (step == 1), 0.375, jnp.where((step == -1) | (step == 2), 0.125, 0.0))


def mean_weights(fine, coarse):
    step = fine - 2 * coarse
    return jnp.where((step == 0) | (step == 1), 0.5, 0.0)


def spread_weights(coarse, fine):
    step = fine - 2 * coarse
    return jnp.where((step == 0) | (step == 1), 0.75, jnp.where((step == -1) | (step == 2), 0.25, 0.0))


def fine_lane(f):
    return signed(f, 256, 192)


def middle_lane(m):
    return signed(m, 128, 96)


def coarse_lane(lane, odd):
    after = jnp.where(lane < 32, lane, jnp.where((lane == 32) & (odd == 1), 4096, lane - odd))
    before = jnp.where((lane == 127) & (odd == 0), 4096, lane - 127 - odd)
    return jnp.where(lane < 64, after, before)


def same_box(coarse, middle, odd):
    edge = 32 * odd
    return (coarse >= edge) == (middle >= 2 * edge)


def restrict_level(plane, coeff, first, count, halve, rows, piece, packed, matrices, store):
    lanes = piece.shape[2]
    parts = packed.shape[2] // lanes
    for j in range(count):
        at = first + 2 * j
        planes = (
            0.375 * (plane(at) + plane(at + 1)) + 0.125 * (plane(at - 1) + plane(at + 2)),
            coeff(at) + coeff(at + 1),
        )
        for kind in range(2):
            for part in range(parts):
                slot = piece.at[(2 * j + kind) * parts + part]
                value = planes[kind][:, lanes * part : lanes * part + lanes]
                packed[kind, pl.ds(rows * j, rows), pl.ds(lanes * part, lanes)] = halve(
                    value, slot, kind == 0
                )
    for kind in range(2):
        result = product(packed[kind], matrices[kind])
        for j in range(count):
            store(kind, j, result[rows * j : rows * j + rows])


def first_kernel(source, conductivity, cells, low, high, done):
    copies = [
        pltpu.make_async_copy(values, cells.at[kind], done.at[kind])
        for kind, values in enumerate((source, conductivity))
    ]
    for copy in copies:
        copy.start()
    for copy in copies:
        copy.wait()
    for kind in range(2):
        for i in range(8):
            low[kind, i] = cells[kind, i, 0:4]
            high[kind, i] = cells[kind, i, 28:32]


def fine_kernel(wide, pair, kept, faces, inverse, rhs, coeff, field, pre, piece, packed):
    lane = lax.broadcasted_iota(jnp.int32, (40, 128), 1)
    edge = (lane < 32) | (lane >= 96)
    for i in range(16):
        halo = wide[2, i]
        rhs[i, :, 0:128] = 2.0 * wide[0, i]
        rhs[i, :, 128:256] = jnp.where(edge, 2.0 * halo, 0.0)
        coeff[i, :, 0:128] = wide[1, i]
        coeff[i, :, 128:256] = jnp.where(edge, pltpu.roll(halo, 64, 1), 0.0)
    operator = Operator(faces)

    def begin(i, value):
        inverse[i] = value
        field[i] = omega_first * rhs[i] * value

    operator.build(plane_of(coeff), 1, 15, begin)

    def store_pre(i, value):
        pre[i] = value
        kept[0, i - 2] = coeff[i]
        kept[1, i - 2] = rhs[i]
        kept[2, i - 2] = value
        kept[3, i - 2] = inverse[i]

    sweep(operator, plane_of(field), plane_of(inverse), plane_of(rhs), omega_second, 2, 14, store_pre)

    def leave(i, applied):
        field[i] = jnp.where(coeff[i] > 0, rhs[i] - applied, 0.0)

    operator.apply(plane_of(pre), 3, 13, leave)
    matrices = (
        lane_map(256, 128, lambda f, c: 4.0 * gather_weights(fine_lane(f), middle_lane(c))),
        lane_map(256, 128, lambda f, c: 0.25 * mean_weights(fine_lane(f), middle_lane(c))),
    )

    def store(kind, j, value):
        pair[kind, j] = value

    restrict_level(plane_of(field), plane_of(coeff), 4, 4, halve_own, 16, piece, packed, matrices, store)


def box_kernel(pair, box, parity, corrected, kept, faces, inverse, field, other, piece, packed, low, low_faces, low_inverse, risen):
    rhs, coeff = plane_of(pair, 0), plane_of(pair, 1)
    operator = Operator(faces)

    def begin(i, value):
        inverse[i] = value
        field[i] = omega_first * rhs(i) * value

    operator.build(coeff, 1, 15, begin)
    sweep(operator, plane_of(field), plane_of(inverse), rhs, omega_second, 2, 14, keep_in(other))

    def leave(i, applied):
        field[i] = jnp.where(coeff(i) > 0, rhs(i) - applied, 0.0)

    operator.apply(plane_of(other), 3, 13, leave)
    odd = parity[0]
    matrices = (
        lane_map(128, 128, lambda m, c: 4.0 * gather_weights(middle_lane(m), coarse_lane(c, odd))),
        lane_map(128, 128, lambda m, c: 0.25 * mean_weights(middle_lane(m), coarse_lane(c, odd))),
    )

    def store(kind, j, value):
        low[kind, j + 1] = value

    restrict_level(plane_of(field), coeff, 4, 4, halve_circular, 24, piece, packed, matrices, store)
    for place in (0, 5):
        for kind in range(3):
            low[kind, place] = jnp.zeros((24, 128), jnp.float32)
    upper, lower = box[0], box[1]
    coarse = BoxOperator(upper, lower, low_faces)

    def begin_low(i, value):
        low_inverse[i] = value
        low[2, i] = omega_first * low[0, i] * value

    coarse.build(plane_of(low, 1), 1, 5, begin_low)

    def store_low(i, value):
        packed[0, pl.ds(24 * (i - 1), 24), :] = value

    sweep(coarse, plane_of(low, 2), plane_of(low_inverse), plane_of(low, 0), omega_second, 1, 5, store_low)

    def spread_box(c, m):
        coarse, fine = coarse_lane(c, odd), middle_lane(m)
        return jnp.where(same_box(coarse, fine, odd), spread_weights(coarse, fine), 0.0)

    result = product(packed[0], lane_map(128, 128, spread_box))
    for j in range(4):
        spread_rows(result[24 * j : 24 * j + 24], risen.at[j], upper, lower)
    for i in range(8):
        value = 0.75 * risen[i // 2]
        near = i // 2 + (1 if i % 2 else -1)
        if 0 <= near < 4:
            value = value + 0.25 * risen[near]
        corrected[i] = near_rows(other[i + 4] + value, 16)
    for kind in range(2):
        for i in range(16):
            kept[kind, i] = near_rows(pair[kind, i], 16)


def spread_rows(values, target, upper=1.0, lower=1.0):
    count = values.shape[0]
    target[pl.ds(0, count, 2), :] = 0.75 * values + 0.25 * (lower * turn(values, 0, -1))
    target[pl.ds(1, count, 2), :] = 0.75 * values + 0.25 * (upper * turn(values, 0, 1))


def face_kernel(pair, filled):
    def take(i, value):
        filled[3, i] = value

    Operator(filled).build(plane_of(pair, 1), 1, 11, take)


def last_kernel(middle, pair, filled, kept, out, faces, field, field_m, packed, risen):
    operator = Operator(filled)
    rhs_m, at_m = plane_of(pair, 0), plane_of(filled, 3)
    sweep(operator, plane_of(middle), at_m, rhs_m, omega_first, 1, 11, keep_in(field_m))

    def store_packed(i, value):
        packed[pl.ds(24 * (i - 2), 24), :] = value

    sweep(operator, plane_of(field_m), at_m, rhs_m, omega_second, 2, 10, store_packed)
    result = product(
        packed[...], lane_map(128, 256, lambda c, f: spread_weights(middle_lane(c), fine_lane(f)))
    )
    for place in range(8):
        for half in range(2):
            spread_rows(
                result[24 * place : 24 * place + 24, 128 * half : 128 * half + 128],
                risen.at[2 * place + half],
            )

    def lifted(place):
        halves = [
            near_rows(risen[2 * place + half], 32) for half in range(2)
        ]
        return jnp.concatenate(halves, axis=1)

    fine = Operator(faces)
    coeff, rhs = plane_of(kept, 0), plane_of(kept, 1)
    fine.build(coeff, 1, 11, None)
    inverse = plane_of(kept, 3)
    for i in range(12):
        place = i // 2 + 1
        value = 0.75 * lifted(place) + 0.25 * lifted(place + (1 if i % 2 else -1))
        field[0, i] = kept[2, i] + jnp.where(coeff(i) > 0, value, 0.0)
    sweep(fine, plane_of(field, 0), inverse, rhs, omega_first, 1, 11, keep_in(field, 1))

    def store_out(i, value):
        out[i - 2] = value[:32, :128]

    sweep(fine, plane_of(field, 1), inverse, rhs, omega_second, 2, 10, store_out)


interpret = False
VMEM = pl.BlockSpec(memory_space=pltpu.VMEM)
SMEM = pl.BlockSpec(memory_space=pltpu.SMEM)
ANY = pl.BlockSpec(memory_space=pl.ANY)


def call(kernel, outs, scratch, *arguments, specs=None):
    return pl.pallas_call(
        kernel,
        out_shape=[jax.ShapeDtypeStruct(shape, jnp.float32) for shape in outs],
        in_specs=specs or [VMEM if value.ndim > 1 else SMEM for value in arguments],
        out_specs=[VMEM] * len(outs),
        scratch_shapes=[
            pltpu.VMEM(shape, jnp.float32) if isinstance(shape, tuple) else shape for shape in scratch
        ],
        compiler_params=pltpu.CompilerParams(vmem_limit_bytes=24 * 1024 * 1024),
        interpret=interpret,
    )(*arguments)


def take_lanes(values, matrix):
    rows = values.reshape(-1, values.shape[-1])
    return lax.dot_general(matrix, rows, (((0,), (1,)), ((), ())), precision=HIGHEST)


def put_lanes(strip, matrix, shape):
    rows = lax.dot_general(strip, matrix, (((0,), (0,)), ((), ())), precision=HIGHEST)
    return rows.reshape(shape)


def local(source, conductivity):
    low_x = lax.axis_index("gx") % 2 == 0
    low_y = lax.axis_index("gy") % 2 == 0
    odd_z = (lax.axis_index("gz") % 2).reshape(1)

    def side(low, when_low, when_high):
        return jnp.where(low, when_low, when_high)

    cells, low, high = call(
        first_kernel,
        [(2, 8, 32, 128), (2, 8, 4, 128), (2, 8, 4, 128)],
        [pltpu.SemaphoreType.DMA((2,))],
        source,
        conductivity,
        specs=[ANY, ANY],
    )
    cells = join([cells, shift(low, "gy", -1), shift(high, "gy", 1)], 2)

    strips = take_lanes(cells, lane_map(128, 64, lambda z, k: z == k + jnp.where(k < 32, 0, 64)))
    after = shift(strips[:32], "gz", -1)
    before = shift(strips[32:], "gz", 1)
    rows = strips.shape[1] // 2
    halo = join([after[:, :rows], before[:, rows:], after[:, rows:], before[:, :rows]], 0)
    halo = put_lanes(halo, lane_map(128, 128, lambda k, z: k == z), (1, 8, 40, 128))
    cells = join([cells, halo], 0)

    far = swap(side(low_x, cells[:, :4], cells[:, 4:]), "gx", True)
    near = swap(side(low_x, cells[:, 4:], cells[:, :4]), "gx", False)
    wide = join([side(low_x, far, near), cells, side(low_x, near, far)], 1)

    plane = (40, 256)
    pair, kept = call(
        fine_kernel,
        [(2, 4, 16, 128), (4, 12, *plane)],
        [(3, 16, *plane)] + [(16, *plane)] * 5 + [(16, 48, 128), (2, 64, 256)],
        wide,
    )

    pair = join([pair, shift(pair, "gy", -1), shift(pair, "gy", 1)], 2)
    far = swap(pair, "gx", True)
    pair = side(low_x, join([far, pair], 1), join([pair, far], 1))
    near = swap(pair, "gx", False)
    pair = side(low_x, join([pair, near], 1), join([near, pair], 1))

    row = lax.broadcasted_iota(jnp.int32, (24, 128), 0)
    edges = side(low_y, row == 23, row == 7), side(low_y, row == 0, row == 8)
    middle, pair = call(
        box_kernel,
        [(8, 24, 128), (2, 16, 24, 128)],
        [(3, 16, 48, 128), (16, 48, 128), (16, 48, 128), (16, 48, 128), (8, 48, 128), (2, 96, 128)]
        + [(3, 6, 24, 128), (4, 6, 24, 128), (6, 24, 128), (4, 48, 128)],
        pair,
        jnp.stack([jnp.where(edge, 0.0, 1.0) for edge in edges]),
        odd_z,
    )

    pair = side(low_x, pair[:, :12], pair[:, 4:])
    (filled,) = call(face_kernel, [(4, 12, 24, 128)], [], pair)
    far = swap(side(low_x, middle[:4], middle[4:]), "gx", True)
    middle = side(low_x, join([far, middle], 0), join([middle, far], 0))

    (pressure,) = call(
        last_kernel,
        [(8, 32, 128)],
        [(3, 12, *plane), (2, 12, *plane), (12, 24, 128), (192, 128), (16, 48, 128)],
        middle,
        pair,
        filled,
        kept,
    )
    return pressure


def solution(mesh):
    spec = P("gx", "gy", "gz")
    return jax.shard_map(local, mesh=mesh, in_specs=(spec, spec), out_specs=spec, check_vma=False)
```

```python
import math

import jax
import jax.numpy as jnp
from jax import lax
from jax.experimental import pallas as pl
from jax.experimental.pallas import tpu as pltpu
from jax.sharding import PartitionSpec as P

spectrum_top = 1.9
spectrum_low = 0.475
mean_value = (spectrum_top + spectrum_low) / 2
half_range = (spectrum_top - spectrum_low) / 2
omega_first = 1.0 / (mean_value + half_range * math.cos(math.pi / 4))
omega_second = 1.0 / (mean_value + half_range * math.cos(3 * math.pi / 4))
HIGHEST = lax.Precision.HIGHEST


def swap(block, axis, outer):
    count = lax.axis_size(axis)
    route = []
    for low in range(1 if outer else 0, count - 1, 2):
        route += [(low, low + 1), (low + 1, low)]
    return lax.ppermute(block, axis, route)


def shift(block, axis, step):
    count = lax.axis_size(axis)
    return lax.ppermute(block, axis, [(i, i + step) for i in range(count) if 0 <= i + step < count])


def cut(values, start, stop, dim):
    return lax.slice_in_dim(values, start, stop, axis=dim)


def join(pieces, dim):
    return jnp.concatenate(pieces, axis=dim)


def turn(plane, dim, step):
    return pltpu.roll(plane, -step % plane.shape[dim], dim)


class Operator:
    def __init__(self, faces):
        self.faces = faces

    def build(self, coeff, start, stop, take):
        before = coeff(start - 1) + coeff(start)
        self.faces[0, start - 1] = before
        for i in range(start, stop):
            here = coeff(i)
            across = here + coeff(i + 1)
            rows = here + turn(here, 0, 1)
            lanes = here + turn(here, 1, 1)
            for place, face in enumerate((across, rows, lanes)):
                self.faces[place, i] = face
            if take is not None:
                diagonal = (across + before) + (rows + turn(rows, 0, -1)) + (lanes + turn(lanes, 1, -1))
                take(i, jnp.where(here > 0, 1.0 / diagonal, 0.0))
            before = across

    def apply(self, field, start, stop, take):
        before = self.faces[0, start - 1] * (field(start - 1) - field(start))
        for i in range(start, stop):
            here = field(i)
            across = self.faces[0, i] * (here - field(i + 1))
            rows = self.faces[1, i] * (here - turn(here, 0, 1))
            lanes = self.faces[2, i] * (here - turn(here, 1, 1))
            take(i, (across - before) + (rows - turn(rows, 0, -1)) + (lanes - turn(lanes, 1, -1)))
            before = across


def sweep(operator, field, inverse, rhs, omega, start, stop, store):
    def take(i, applied):
        store(i, field(i) + (omega * (rhs(i) - applied)) * inverse(i))

    operator.apply(field, start, stop, take)


class BoxOperator:
    def __init__(self, upper, lower, faces):
        self.upper = upper
        self.lower = lower
        self.faces = faces

    def build(self, coeff, start, stop, take):
        before = coeff(start - 1) + coeff(start)
        self.faces[0, start - 1] = before
        for i in range(start, stop):
            here = coeff(i)
            across = here + coeff(i + 1)
            rows = here + self.upper * turn(here, 0, 1)
            back = here + self.lower * turn(here, 0, -1)
            lanes = here + turn(here, 1, 1)
            for place, face in enumerate((across, rows, lanes, back)):
                self.faces[place, i] = face
            diagonal = (across + before) + (rows + back) + (lanes + turn(lanes, 1, -1))
            take(i, jnp.where(here > 0, 1.0 / diagonal, 0.0))
            before = across

    def apply(self, field, start, stop, take):
        before = self.faces[0, start - 1] * (field(start - 1) - field(start))
        for i in range(start, stop):
            here = field(i)
            across = self.faces[0, i] * (here - field(i + 1))
            rows = self.faces[1, i] * (here - self.upper * turn(here, 0, 1))
            back = self.faces[3, i] * (here - self.lower * turn(here, 0, -1))
            lanes = self.faces[2, i] * (here - turn(here, 1, 1))
            take(i, (across - before) + (rows + back) + (lanes - turn(lanes, 1, -1)))
            before = across


def plane_of(ref, *lead):
    return lambda i: ref[(*lead, i)]


def keep_in(ref, *lead):
    def store(i, value):
        ref[(*lead, i)] = value

    return store


def halve_circular(plane, slot, weights):
    count = plane.shape[0] // 2
    slot[...] = plane
    even = slot[pl.ds(0, count, 2), :]
    odd = slot[pl.ds(1, count, 2), :]
    if not weights:
        return even + odd
    return 0.375 * (even + odd) + 0.125 * (turn(odd, 0, -1) + turn(even, 0, 1))


def halve_own(plane, slot, weights):
    slot[0:8] = plane[32:40]
    slot[8:40] = plane[0:32]
    slot[40:48] = plane[32:40]
    even = slot[pl.ds(8, 16, 2), :]
    odd = slot[pl.ds(9, 16, 2), :]
    if not weights:
        return even + odd
    return 0.375 * (even + odd) + 0.125 * (slot[pl.ds(7, 16, 2), :] + slot[pl.ds(10, 16, 2), :])


def near_rows(plane, own):
    row = lax.broadcasted_iota(jnp.int32, (8, plane.shape[1]), 0)
    edge = jnp.where(row < 4, plane[own : own + 8], plane[plane.shape[0] - 8 :])
    return jnp.concatenate([plane[:own], edge], axis=0)


def product(values, matrix):
    return jnp.dot(values, matrix, precision=HIGHEST, preferred_element_type=jnp.float32)


def lane_map(rows, columns, entries):
    row = lax.broadcasted_iota(jnp.int32, (rows, columns), 0)
    column = lax.broadcasted_iota(jnp.int32, (rows, columns), 1)
    return entries(row, column).astype(jnp.float32)


def signed(index, size, after):
    return jnp.where(index < after, index, index - size)


def gather_weights(fine, coarse):
    step = fine - 2 * coarse
    return jnp.where((step == 0) | (step == 1), 0.375, jnp.where((step == -1) | (step == 2), 0.125, 0.0))


def mean_weights(fine, coarse):
    step = fine - 2 * coarse
    return jnp.where((step == 0) | (step == 1), 0.5, 0.0)


def spread_weights(coarse, fine):
    step = fine - 2 * coarse
    return jnp.where((step == 0) | (step == 1), 0.75, jnp.where((step == -1) | (step == 2), 0.25, 0.0))


def fine_lane(f):
    return signed(f, 256, 192)


def middle_lane(m):
    return signed(m, 128, 96)


def coarse_lane(lane, odd):
    after = jnp.where(lane < 32, lane, jnp.where((lane == 32) & (odd == 1), 4096, lane - odd))
    before = jnp.where((lane == 127) & (odd == 0), 4096, lane - 127 - odd)
    return jnp.where(lane < 64, after, before)


def same_box(coarse, middle, odd):
    edge = 32 * odd
    return (coarse >= edge) == (middle >= 2 * edge)


def restrict_level(plane, coeff, first, count, halve, rows, piece, packed, matrices, store):
    lanes = piece.shape[2]
    parts = packed.shape[2] // lanes
    for j in range(count):
        at = first + 2 * j
        planes = (
            0.375 * (plane(at) + plane(at + 1)) + 0.125 * (plane(at - 1) + plane(at + 2)),
            coeff(at) + coeff(at + 1),
        )
        for kind in range(2):
            for part in range(parts):
                slot = piece.at[(2 * j + kind) * parts + part]
                value = planes[kind][:, lanes * part : lanes * part + lanes]
                packed[kind, pl.ds(rows * j, rows), pl.ds(lanes * part, lanes)] = halve(
                    value, slot, kind == 0
                )
    for kind in range(2):
        result = product(packed[kind], matrices[kind])
        for j in range(count):
            store(kind, j, result[rows * j : rows * j + rows])


class Joined:
    def __init__(self, own, scratch):
        self.own = own
        self.scratch = scratch

    def __getitem__(self, place):
        lead, i = place[:-1], place[-1]
        return self.own[(*lead, i - 4)] if 5 <= i <= 10 else self.scratch[place]

    def __setitem__(self, place, value):
        self.scratch[place] = value


def halo_edge():
    lane = lax.broadcasted_iota(jnp.int32, (40, 128), 1)
    return (lane < 32) | (lane >= 96)


def stage_coeff(cells, coeff, i):
    coeff[i, :, 0:128] = cells[1, i]
    coeff[i, :, 128:256] = jnp.where(halo_edge(), pltpu.roll(cells[2, i], 64, 1), 0.0)


def own_kernel(cells, faces, inverse, coeff):
    for i in range(8):
        stage_coeff(cells, coeff, i)
    Operator(faces).build(plane_of(coeff), 1, 7, keep_in(inverse))


def fine_kernel(wide, own_faces, own_inverse, pair, kept, faces, inverse, rhs, coeff, field, pre, piece, packed):
    for i in range(16):
        rhs[i, :, 0:128] = 2.0 * wide[0, i]
        rhs[i, :, 128:256] = jnp.where(halo_edge(), 2.0 * wide[2, i], 0.0)
        stage_coeff(wide, coeff, i)
    operator = Operator(Joined(own_faces, faces))
    scratch, inverse = inverse, plane_of(Joined(own_inverse, inverse))
    operator.build(plane_of(coeff), 1, 5, keep_in(scratch))
    operator.build(plane_of(coeff), 11, 15, keep_in(scratch))
    for i in range(1, 15):
        field[i] = omega_first * rhs[i] * inverse(i)

    def store_pre(i, value):
        pre[i] = value
        kept[0, i - 2] = coeff[i]
        kept[1, i - 2] = rhs[i]
        kept[2, i - 2] = value
        kept[3, i - 2] = inverse(i)

    sweep(operator, plane_of(field), inverse, plane_of(rhs), omega_second, 2, 14, store_pre)

    def leave(i, applied):
        field[i] = jnp.where(coeff[i] > 0, rhs[i] - applied, 0.0)

    operator.apply(plane_of(pre), 3, 13, leave)
    matrices = (
        lane_map(256, 128, lambda f, c: 4.0 * gather_weights(fine_lane(f), middle_lane(c))),
        lane_map(256, 128, lambda f, c: 0.25 * mean_weights(fine_lane(f), middle_lane(c))),
    )

    def store(kind, j, value):
        pair[kind, j] = value

    restrict_level(plane_of(field), plane_of(coeff), 4, 4, halve_own, 16, piece, packed, matrices, store)


def box_kernel(pair, box, parity, corrected, kept, faces, inverse, field, other, piece, packed, low, low_faces, low_inverse, risen):
    rhs, coeff = plane_of(pair, 0), plane_of(pair, 1)
    operator = Operator(faces)

    def begin(i, value):
        inverse[i] = value
        field[i] = omega_first * rhs(i) * value

    operator.build(coeff, 1, 15, begin)
    sweep(operator, plane_of(field), plane_of(inverse), rhs, omega_second, 2, 14, keep_in(other))

    def leave(i, applied):
        field[i] = jnp.where(coeff(i) > 0, rhs(i) - applied, 0.0)

    operator.apply(plane_of(other), 3, 13, leave)
    odd = parity[0]
    matrices = (
        lane_map(128, 128, lambda m, c: 4.0 * gather_weights(middle_lane(m), coarse_lane(c, odd))),
        lane_map(128, 128, lambda m, c: 0.25 * mean_weights(middle_lane(m), coarse_lane(c, odd))),
    )

    def store(kind, j, value):
        low[kind, j + 1] = value

    restrict_level(plane_of(field), coeff, 4, 4, halve_circular, 24, piece, packed, matrices, store)
    for place in (0, 5):
        for kind in range(3):
            low[kind, place] = jnp.zeros((24, 128), jnp.float32)
    upper, lower = box[0], box[1]
    coarse = BoxOperator(upper, lower, low_faces)

    def begin_low(i, value):
        low_inverse[i] = value
        low[2, i] = omega_first * low[0, i] * value

    coarse.build(plane_of(low, 1), 1, 5, begin_low)

    def store_low(i, value):
        packed[0, pl.ds(24 * (i - 1), 24), :] = value

    sweep(coarse, plane_of(low, 2), plane_of(low_inverse), plane_of(low, 0), omega_second, 1, 5, store_low)

    def spread_box(c, m):
        coarse, fine = coarse_lane(c, odd), middle_lane(m)
        return jnp.where(same_box(coarse, fine, odd), spread_weights(coarse, fine), 0.0)

    result = product(packed[0], lane_map(128, 128, spread_box))
    for j in range(4):
        spread_rows(result[24 * j : 24 * j + 24], risen.at[j], upper, lower)
    for i in range(8):
        value = 0.75 * risen[i // 2]
        near = i // 2 + (1 if i % 2 else -1)
        if 0 <= near < 4:
            value = value + 0.25 * risen[near]
        corrected[i] = near_rows(other[i + 4] + value, 16)
    for kind in range(2):
        for i in range(16):
            kept[kind, i] = near_rows(pair[kind, i], 16)


def spread_rows(values, target, upper=1.0, lower=1.0):
    count = values.shape[0]
    target[pl.ds(0, count, 2), :] = 0.75 * values + 0.25 * (lower * turn(values, 0, -1))
    target[pl.ds(1, count, 2), :] = 0.75 * values + 0.25 * (upper * turn(values, 0, 1))


def face_kernel(pair, filled):
    def take(i, value):
        filled[3, i] = value

    Operator(filled).build(plane_of(pair, 1), 1, 11, take)


def last_kernel(middle, pair, filled, kept, out, faces, field, field_m, packed, risen):
    operator = Operator(filled)
    rhs_m, at_m = plane_of(pair, 0), plane_of(filled, 3)
    sweep(operator, plane_of(middle), at_m, rhs_m, omega_first, 1, 11, keep_in(field_m))

    def store_packed(i, value):
        packed[pl.ds(24 * (i - 2), 24), :] = value

    sweep(operator, plane_of(field_m), at_m, rhs_m, omega_second, 2, 10, store_packed)
    result = product(
        packed[...], lane_map(128, 256, lambda c, f: spread_weights(middle_lane(c), fine_lane(f)))
    )
    for place in range(8):
        for half in range(2):
            spread_rows(
                result[24 * place : 24 * place + 24, 128 * half : 128 * half + 128],
                risen.at[2 * place + half],
            )

    def lifted(place):
        halves = [
            near_rows(risen[2 * place + half], 32) for half in range(2)
        ]
        return jnp.concatenate(halves, axis=1)

    fine = Operator(faces)
    coeff, rhs = plane_of(kept, 0), plane_of(kept, 1)
    fine.build(coeff, 1, 11, None)
    inverse = plane_of(kept, 3)
    for i in range(12):
        place = i // 2 + 1
        value = 0.75 * lifted(place) + 0.25 * lifted(place + (1 if i % 2 else -1))
        field[0, i] = kept[2, i] + jnp.where(coeff(i) > 0, value, 0.0)
    sweep(fine, plane_of(field, 0), inverse, rhs, omega_first, 1, 11, keep_in(field, 1))

    def store_out(i, value):
        out[i - 2] = value[:32, :128]

    sweep(fine, plane_of(field, 1), inverse, rhs, omega_second, 2, 10, store_out)


interpret = False
VMEM = pl.BlockSpec(memory_space=pltpu.VMEM)
SMEM = pl.BlockSpec(memory_space=pltpu.SMEM)
HBM = pl.BlockSpec(memory_space=pltpu.HBM)


def call(kernel, outs, scratch, *arguments, specs=None):
    return pl.pallas_call(
        kernel,
        out_shape=[jax.ShapeDtypeStruct(shape, jnp.float32) for shape in outs],
        in_specs=specs or [VMEM if value.ndim > 1 else SMEM for value in arguments],
        out_specs=[VMEM] * len(outs),
        scratch_shapes=[
            pltpu.VMEM(shape, jnp.float32) if isinstance(shape, tuple) else shape for shape in scratch
        ],
        compiler_params=pltpu.CompilerParams(vmem_limit_bytes=24 * 1024 * 1024),
        interpret=interpret,
    )(*arguments)


def take_lanes(values, matrix):
    rows = values.reshape(-1, values.shape[-1])
    return lax.dot_general(matrix, rows, (((0,), (1,)), ((), ())), precision=HIGHEST)


def put_lanes(strip, matrix, shape):
    rows = lax.dot_general(strip, matrix, (((0,), (0,)), ((), ())), precision=HIGHEST)
    return rows.reshape(shape)


def local(source, conductivity):
    low_x = lax.axis_index("gx") % 2 == 0
    low_y = lax.axis_index("gy") % 2 == 0
    odd_z = (lax.axis_index("gz") % 2).reshape(1)

    def side(low, when_low, when_high):
        return jnp.where(low, when_low, when_high)

    cells = jnp.stack([source, conductivity])
    low, high = cells[:, :, :4], cells[:, :, 28:]
    cells = lax.optimization_barrier(cells)
    cells = join([cells, shift(low, "gy", -1), shift(high, "gy", 1)], 2)

    strips = take_lanes(cells, lane_map(128, 64, lambda z, k: z == k + jnp.where(k < 32, 0, 64)))
    after = shift(strips[:32], "gz", -1)
    before = shift(strips[32:], "gz", 1)
    rows = strips.shape[1] // 2
    halo = join([after[:, :rows], before[:, rows:], after[:, rows:], before[:, :rows]], 0)
    halo = put_lanes(halo, lane_map(128, 128, lambda k, z: k == z), (1, 8, 40, 128))
    cells = join([cells, halo], 0)

    own = call(own_kernel, [(3, 8, 40, 256), (8, 40, 256)], [(8, 40, 256)], cells)
    far = swap(side(low_x, cells[:, :4], cells[:, 4:]), "gx", True)
    near = swap(side(low_x, cells[:, 4:], cells[:, :4]), "gx", False)
    wide = join([side(low_x, far, near), cells, side(low_x, near, far)], 1)

    plane = (40, 256)
    pair, kept = call(
        fine_kernel,
        [(2, 4, 16, 128), (4, 12, *plane)],
        [(3, 16, *plane)] + [(16, *plane)] * 5 + [(16, 48, 128), (2, 64, 256)],
        wide,
        *own,
    )

    pair = join([pair, shift(pair, "gy", -1), shift(pair, "gy", 1)], 2)
    far = swap(pair, "gx", True)
    pair = side(low_x, join([far, pair], 1), join([pair, far], 1))
    near = swap(pair, "gx", False)
    pair = side(low_x, join([pair, near], 1), join([near, pair], 1))

    row = lax.broadcasted_iota(jnp.int32, (24, 128), 0)
    edges = side(low_y, row == 23, row == 7), side(low_y, row == 0, row == 8)
    middle, pair = call(
        box_kernel,
        [(8, 24, 128), (2, 16, 24, 128)],
        [(3, 16, 48, 128), (16, 48, 128), (16, 48, 128), (16, 48, 128), (8, 48, 128), (2, 96, 128)]
        + [(3, 6, 24, 128), (4, 6, 24, 128), (6, 24, 128), (4, 48, 128)],
        pair,
        jnp.stack([jnp.where(edge, 0.0, 1.0) for edge in edges]),
        odd_z,
    )

    pair = side(low_x, pair[:, :12], pair[:, 4:])
    (filled,) = call(face_kernel, [(4, 12, 24, 128)], [], pair)
    far = swap(side(low_x, middle[:4], middle[4:]), "gx", True)
    middle = side(low_x, join([far, middle], 0), join([middle, far], 0))

    (pressure,) = call(
        last_kernel,
        [(8, 32, 128)],
        [(3, 12, *plane), (2, 12, *plane), (12, 24, 128), (192, 128), (16, 48, 128)],
        middle,
        pair,
        filled,
        kept,
    )
    return pressure


def solution(mesh):
    spec = P("gx", "gy", "gz")
    return jax.shard_map(local, mesh=mesh, in_specs=(spec, spec), out_specs=spec, check_vma=False)
```

```python
import math

import jax
import jax.numpy as jnp
from jax import lax
from jax.experimental import pallas as pl
from jax.experimental.pallas import tpu as pltpu
from jax.sharding import PartitionSpec as P

spectrum_top = 1.9
spectrum_low = 0.475
mean_value = (spectrum_top + spectrum_low) / 2
half_range = (spectrum_top - spectrum_low) / 2
omega_first = 1.0 / (mean_value + half_range * math.cos(math.pi / 4))
omega_second = 1.0 / (mean_value + half_range * math.cos(3 * math.pi / 4))
HIGHEST = lax.Precision.HIGHEST


def swap(block, axis, outer):
    count = lax.axis_size(axis)
    route = []
    for low in range(1 if outer else 0, count - 1, 2):
        route += [(low, low + 1), (low + 1, low)]
    return lax.ppermute(block, axis, route)


def shift(block, axis, step):
    count = lax.axis_size(axis)
    return lax.ppermute(block, axis, [(i, i + step) for i in range(count) if 0 <= i + step < count])


def cut(values, start, stop, dim):
    return lax.slice_in_dim(values, start, stop, axis=dim)


def join(pieces, dim):
    return jnp.concatenate(pieces, axis=dim)


def turn(plane, dim, step):
    return pltpu.roll(plane, -step % plane.shape[dim], dim)


class Operator:
    def __init__(self, faces):
        self.faces = faces

    def build(self, coeff, start, stop, take):
        before = coeff(start - 1) + coeff(start)
        self.faces[0, start - 1] = before
        for i in range(start, stop):
            here = coeff(i)
            across = here + coeff(i + 1)
            rows = here + turn(here, 0, 1)
            lanes = here + turn(here, 1, 1)
            for place, face in enumerate((across, rows, lanes)):
                self.faces[place, i] = face
            if take is not None:
                diagonal = (across + before) + (rows + turn(rows, 0, -1)) + (lanes + turn(lanes, 1, -1))
                take(i, jnp.where(here > 0, 1.0 / diagonal, 0.0))
            before = across

    def apply(self, field, start, stop, take):
        before = self.faces[0, start - 1] * (field(start - 1) - field(start))
        for i in range(start, stop):
            here = field(i)
            across = self.faces[0, i] * (here - field(i + 1))
            rows = self.faces[1, i] * (here - turn(here, 0, 1))
            lanes = self.faces[2, i] * (here - turn(here, 1, 1))
            take(i, (across - before) + (rows - turn(rows, 0, -1)) + (lanes - turn(lanes, 1, -1)))
            before = across


def sweep(operator, field, inverse, rhs, omega, start, stop, store):
    def take(i, applied):
        store(i, field(i) + (omega * (rhs(i) - applied)) * inverse(i))

    operator.apply(field, start, stop, take)


class BoxOperator:
    def __init__(self, upper, lower, faces):
        self.upper = upper
        self.lower = lower
        self.faces = faces

    def build(self, coeff, start, stop, take):
        before = coeff(start - 1) + coeff(start)
        self.faces[0, start - 1] = before
        for i in range(start, stop):
            here = coeff(i)
            across = here + coeff(i + 1)
            rows = here + self.upper * turn(here, 0, 1)
            back = here + self.lower * turn(here, 0, -1)
            lanes = here + turn(here, 1, 1)
            for place, face in enumerate((across, rows, lanes, back)):
                self.faces[place, i] = face
            diagonal = (across + before) + (rows + back) + (lanes + turn(lanes, 1, -1))
            take(i, jnp.where(here > 0, 1.0 / diagonal, 0.0))
            before = across

    def apply(self, field, start, stop, take):
        before = self.faces[0, start - 1] * (field(start - 1) - field(start))
        for i in range(start, stop):
            here = field(i)
            across = self.faces[0, i] * (here - field(i + 1))
            rows = self.faces[1, i] * (here - self.upper * turn(here, 0, 1))
            back = self.faces[3, i] * (here - self.lower * turn(here, 0, -1))
            lanes = self.faces[2, i] * (here - turn(here, 1, 1))
            take(i, (across - before) + (rows + back) + (lanes - turn(lanes, 1, -1)))
            before = across


def plane_of(ref, *lead):
    return lambda i: ref[(*lead, i)]


def keep_in(ref, *lead):
    def store(i, value):
        ref[(*lead, i)] = value

    return store


def halve_circular(plane, slot, weights):
    count = plane.shape[0] // 2
    slot[...] = plane
    even = slot[pl.ds(0, count, 2), :]
    odd = slot[pl.ds(1, count, 2), :]
    if not weights:
        return even + odd
    return 0.375 * (even + odd) + 0.125 * (turn(odd, 0, -1) + turn(even, 0, 1))


def halve_own(plane, slot, weights):
    slot[0:8] = plane[32:40]
    slot[8:40] = plane[0:32]
    slot[40:48] = plane[32:40]
    even = slot[pl.ds(8, 16, 2), :]
    odd = slot[pl.ds(9, 16, 2), :]
    if not weights:
        return even + odd
    return 0.375 * (even + odd) + 0.125 * (slot[pl.ds(7, 16, 2), :] + slot[pl.ds(10, 16, 2), :])


def near_rows(plane, own):
    row = lax.broadcasted_iota(jnp.int32, (8, plane.shape[1]), 0)
    edge = jnp.where(row < 4, plane[own : own + 8], plane[plane.shape[0] - 8 :])
    return jnp.concatenate([plane[:own], edge], axis=0)


def product(values, matrix):
    return jnp.dot(values, matrix, precision=HIGHEST, preferred_element_type=jnp.float32)


def lane_map(rows, columns, entries):
    row = lax.broadcasted_iota(jnp.int32, (rows, columns), 0)
    column = lax.broadcasted_iota(jnp.int32, (rows, columns), 1)
    return entries(row, column).astype(jnp.float32)


def signed(index, size, after):
    return jnp.where(index < after, index, index - size)


def gather_weights(fine, coarse):
    step = fine - 2 * coarse
    return jnp.where((step == 0) | (step == 1), 0.375, jnp.where((step == -1) | (step == 2), 0.125, 0.0))


def mean_weights(fine, coarse):
    step = fine - 2 * coarse
    return jnp.where((step == 0) | (step == 1), 0.5, 0.0)


def spread_weights(coarse, fine):
    step = fine - 2 * coarse
    return jnp.where((step == 0) | (step == 1), 0.75, jnp.where((step == -1) | (step == 2), 0.25, 0.0))


def fine_lane(f):
    return signed(f, 256, 192)


def middle_lane(m):
    return signed(m, 128, 96)


def coarse_lane(lane, odd):
    after = jnp.where(lane < 32, lane, jnp.where((lane == 32) & (odd == 1), 4096, lane - odd))
    before = jnp.where((lane == 127) & (odd == 0), 4096, lane - 127 - odd)
    return jnp.where(lane < 64, after, before)


def same_box(coarse, middle, odd):
    edge = 32 * odd
    return (coarse >= edge) == (middle >= 2 * edge)


def between(plane, at):
    return 0.375 * (plane(at) + plane(at + 1)) + 0.125 * (plane(at - 1) + plane(at + 2))


def both(plane, at):
    return plane(at) + plane(at + 1)


def restrict_level(weights, plane, first, halve, rows, piece, packed, matrix, store):
    lanes = piece.shape[2]
    parts = packed.shape[1] // lanes
    for j in range(4):
        value = (between if weights else both)(plane, first + 2 * j)
        for part in range(parts):
            packed[pl.ds(rows * j, rows), pl.ds(lanes * part, lanes)] = halve(
                value[:, lanes * part : lanes * part + lanes], piece.at[j * parts + part], weights
            )
    result = product(packed[...], matrix)
    for j in range(4):
        store(j, result[rows * j : rows * j + rows])


class Joined:
    def __init__(self, own, scratch, first, last, start):
        self.own = own
        self.scratch = scratch
        self.planes = first, last, start

    def __getitem__(self, place):
        first, last, start = self.planes
        lead, i = place[:-1], place[-1]
        return self.own[(*lead, i - start)] if first <= i <= last else self.scratch[place]

    def __setitem__(self, place, value):
        self.scratch[place] = value


def halo_edge():
    lane = lax.broadcasted_iota(jnp.int32, (40, 128), 1)
    return (lane < 32) | (lane >= 96)


def stage(cells, rhs, coeff, i):
    edge = halo_edge()
    rhs[i, :, 0:128] = 2.0 * cells[0, i]
    rhs[i, :, 128:256] = jnp.where(edge, 2.0 * cells[2, i], 0.0)
    coeff[i, :, 0:128] = cells[1, i]
    coeff[i, :, 128:256] = jnp.where(edge, pltpu.roll(cells[2, i], 64, 1), 0.0)


def own_kernel(cells, faces, inverse, pre, left, middle_coeff, rhs, coeff, field, piece, packed):
    for i in range(8):
        stage(cells, rhs, coeff, i)
    operator = Operator(faces)

    def begin(i, value):
        inverse[i] = value
        field[i] = omega_first * rhs[i] * value

    operator.build(plane_of(coeff), 1, 7, begin)

    def store_pre(i, value):
        pre[i - 2] = value

    sweep(operator, plane_of(field), plane_of(inverse), plane_of(rhs), omega_second, 2, 6, store_pre)

    def leave(i, applied):
        left[i - 3] = jnp.where(coeff[i] > 0, rhs[i] - applied, 0.0)

    operator.apply(lambda i: pre[i - 2], 3, 5, leave)
    matrix = lane_map(256, 128, lambda f, c: 0.25 * mean_weights(fine_lane(f), middle_lane(c)))
    restrict_level(
        False, plane_of(coeff), 0, halve_own, 16, piece, packed, matrix, keep_in(middle_coeff)
    )


def fine_kernel(
    wide, own_faces, own_inverse, own_pre, own_left, own_coeff,
    pair, kept, faces, inverse, rhs, coeff, field, pre, left, piece, packed,
):
    for i in range(16):
        stage(wide, rhs, coeff, i)
    operator = Operator(Joined(own_faces, faces, 5, 10, 4))
    for start in (1, 11):
        operator.build(plane_of(coeff), start, start + 4, keep_in(inverse))
    inverses = plane_of(Joined(own_inverse, inverse, 5, 10, 4))
    smoothed = plane_of(Joined(own_pre, pre, 6, 9, 6))
    leftover = plane_of(Joined(own_left, left, 7, 8, 7))
    for i in (*range(1, 7), *range(9, 15)):
        field[i] = omega_first * rhs[i] * inverses(i)
    for start in (2, 10):
        sweep(
            operator, plane_of(field), inverses, plane_of(rhs), omega_second, start, start + 4, keep_in(pre)
        )
    for i in range(2, 14):
        for kind, plane in enumerate((plane_of(coeff), plane_of(rhs), smoothed, inverses)):
            kept[kind, i - 2] = plane(i)

    def leave(i, applied):
        left[i] = jnp.where(coeff[i] > 0, rhs[i] - applied, 0.0)

    for start in (3, 9):
        operator.apply(smoothed, start, start + 4, leave)
    matrix = lane_map(256, 128, lambda f, c: 4.0 * gather_weights(fine_lane(f), middle_lane(c)))
    restrict_level(True, leftover, 4, halve_own, 16, piece, packed, matrix, keep_in(pair, 0))
    for j in range(4):
        pair[1, j] = own_coeff[j]


def box_kernel(narrow, box, parity, corrected, kept, pair, faces, inverse, field, other, piece, packed, low, low_faces, low_inverse, risen):
    after = lax.broadcasted_iota(jnp.int32, (8, 128), 0) < 4
    for kind in range(2):
        for i in range(16):
            pair[kind, i, 0:24] = narrow[kind, i, 0:24]
            pair[kind, i, 24:32] = jnp.where(after, narrow[kind, i, 24:32], 0.0)
            pair[kind, i, 32:40] = jnp.where(after, 0.0, narrow[kind, i, 24:32])
            pair[kind, i, 40:48] = narrow[kind, i, 32:40]
    rhs, coeff = plane_of(pair, 0), plane_of(pair, 1)
    operator = Operator(faces)

    def begin(i, value):
        inverse[i] = value
        field[i] = omega_first * rhs(i) * value

    operator.build(coeff, 1, 15, begin)
    sweep(operator, plane_of(field), plane_of(inverse), rhs, omega_second, 2, 14, keep_in(other))

    def leave(i, applied):
        field[i] = jnp.where(coeff(i) > 0, rhs(i) - applied, 0.0)

    operator.apply(plane_of(other), 3, 13, leave)
    odd = parity[0]
    for kind, matrix in enumerate(
        (
            lane_map(128, 128, lambda m, c: 4.0 * gather_weights(middle_lane(m), coarse_lane(c, odd))),
            lane_map(128, 128, lambda m, c: 0.25 * mean_weights(middle_lane(m), coarse_lane(c, odd))),
        )
    ):

        def store(j, value, kind=kind):
            low[kind, j + 1] = value

        plane = coeff if kind else plane_of(field)
        restrict_level(kind == 0, plane, 4, halve_circular, 24, piece.at[kind], packed.at[kind], matrix, store)
    for place in (0, 5):
        for kind in range(3):
            low[kind, place] = jnp.zeros((24, 128), jnp.float32)
    upper, lower = box[0], box[1]
    coarse = BoxOperator(upper, lower, low_faces)

    def begin_low(i, value):
        low_inverse[i] = value
        low[2, i] = omega_first * low[0, i] * value

    coarse.build(plane_of(low, 1), 1, 5, begin_low)

    def store_low(i, value):
        packed[0, pl.ds(24 * (i - 1), 24), :] = value

    sweep(coarse, plane_of(low, 2), plane_of(low_inverse), plane_of(low, 0), omega_second, 1, 5, store_low)

    def spread_box(c, m):
        coarse, fine = coarse_lane(c, odd), middle_lane(m)
        return jnp.where(same_box(coarse, fine, odd), spread_weights(coarse, fine), 0.0)

    result = product(packed[0], lane_map(128, 128, spread_box))
    for j in range(4):
        spread_rows(result[24 * j : 24 * j + 24], risen.at[j], upper, lower)
    for i in range(8):
        value = 0.75 * risen[i // 2]
        near = i // 2 + (1 if i % 2 else -1)
        if 0 <= near < 4:
            value = value + 0.25 * risen[near]
        corrected[i] = near_rows(other[i + 4] + value, 16)
    for kind in range(2):
        for i in range(16):
            kept[kind, i] = near_rows(pair[kind, i], 16)


def spread_rows(values, target, upper=1.0, lower=1.0):
    count = values.shape[0]
    target[pl.ds(0, count, 2), :] = 0.75 * values + 0.25 * (lower * turn(values, 0, -1))
    target[pl.ds(1, count, 2), :] = 0.75 * values + 0.25 * (upper * turn(values, 0, 1))


def face_kernel(pair, filled):
    def take(i, value):
        filled[3, i] = value

    Operator(filled).build(plane_of(pair, 1), 1, 11, take)


def last_kernel(middle, pair, filled, kept, out, faces, field, field_m, packed, risen):
    operator = Operator(filled)
    rhs_m, at_m = plane_of(pair, 0), plane_of(filled, 3)
    sweep(operator, plane_of(middle), at_m, rhs_m, omega_first, 1, 11, keep_in(field_m))

    def store_packed(i, value):
        packed[pl.ds(24 * (i - 2), 24), :] = value

    sweep(operator, plane_of(field_m), at_m, rhs_m, omega_second, 2, 10, store_packed)
    result = product(
        packed[...], lane_map(128, 256, lambda c, f: spread_weights(middle_lane(c), fine_lane(f)))
    )
    for place in range(8):
        for half in range(2):
            spread_rows(
                result[24 * place : 24 * place + 24, 128 * half : 128 * half + 128],
                risen.at[2 * place + half],
            )

    def lifted(place):
        halves = [
            near_rows(risen[2 * place + half], 32) for half in range(2)
        ]
        return jnp.concatenate(halves, axis=1)

    fine = Operator(faces)
    coeff, rhs = plane_of(kept, 0), plane_of(kept, 1)
    fine.build(coeff, 1, 11, None)
    inverse = plane_of(kept, 3)
    for i in range(12):
        place = i // 2 + 1
        value = 0.75 * lifted(place) + 0.25 * lifted(place + (1 if i % 2 else -1))
        field[0, i] = kept[2, i] + jnp.where(coeff(i) > 0, value, 0.0)
    sweep(fine, plane_of(field, 0), inverse, rhs, omega_first, 1, 11, keep_in(field, 1))

    def store_out(i, value):
        out[i - 2] = value[:32, :128]

    sweep(fine, plane_of(field, 1), inverse, rhs, omega_second, 2, 10, store_out)


interpret = False
VMEM = pl.BlockSpec(memory_space=pltpu.VMEM)
SMEM = pl.BlockSpec(memory_space=pltpu.SMEM)
HBM = pl.BlockSpec(memory_space=pltpu.HBM)


def call(kernel, outs, scratch, *arguments, specs=None):
    return pl.pallas_call(
        kernel,
        out_shape=[jax.ShapeDtypeStruct(shape, jnp.float32) for shape in outs],
        in_specs=specs or [VMEM if value.ndim > 1 else SMEM for value in arguments],
        out_specs=[VMEM] * len(outs),
        scratch_shapes=[
            pltpu.VMEM(shape, jnp.float32) if isinstance(shape, tuple) else shape for shape in scratch
        ],
        compiler_params=pltpu.CompilerParams(vmem_limit_bytes=24 * 1024 * 1024),
        interpret=interpret,
    )(*arguments)


def take_lanes(values, matrix):
    rows = values.reshape(-1, values.shape[-1])
    return lax.dot_general(matrix, rows, (((0,), (1,)), ((), ())), precision=HIGHEST)


def put_lanes(strip, matrix, shape):
    rows = lax.dot_general(strip, matrix, (((0,), (0,)), ((), ())), precision=HIGHEST)
    return rows.reshape(shape)


def local(source, conductivity):
    low_x = lax.axis_index("gx") % 2 == 0
    low_y = lax.axis_index("gy") % 2 == 0
    odd_z = (lax.axis_index("gz") % 2).reshape(1)

    def side(low, when_low, when_high):
        return jnp.where(low, when_low, when_high)

    cells = jnp.stack([source, conductivity])
    low, high = cells[:, :, :4], cells[:, :, 28:]
    cells = lax.optimization_barrier(cells)
    cells = join([cells, shift(low, "gy", -1), shift(high, "gy", 1)], 2)

    strips = take_lanes(cells, lane_map(128, 64, lambda z, k: z == k + jnp.where(k < 32, 0, 64)))
    after = shift(strips[:32], "gz", -1)
    before = shift(strips[32:], "gz", 1)
    rows = strips.shape[1] // 2
    halo = join([after[:, :rows], before[:, rows:], after[:, rows:], before[:, :rows]], 0)
    halo = put_lanes(halo, lane_map(128, 128, lambda k, z: k == z), (1, 8, 40, 128))
    cells = join([cells, halo], 0)

    plane = (40, 256)
    own = call(
        own_kernel,
        [(3, 8, *plane), (8, *plane), (4, *plane), (2, *plane), (4, 16, 128)],
        [(8, *plane), (8, *plane), (8, *plane), (8, 48, 128), (64, 256)],
        cells,
    )
    far = swap(side(low_x, cells[:, :4], cells[:, 4:]), "gx", True)
    near = swap(side(low_x, cells[:, 4:], cells[:, :4]), "gx", False)
    wide = join([side(low_x, far, near), cells, side(low_x, near, far)], 1)

    pair, kept = call(
        fine_kernel,
        [(2, 4, 16, 128), (4, 12, *plane)],
        [(3, 16, *plane)] + [(16, *plane)] * 6 + [(8, 48, 128), (64, 256)],
        wide,
        *own,
    )

    after, before = shift(pair, "gy", -1), shift(pair, "gy", 1)
    pair = join([pair, after[:, :, :12], before[:, :, 4:]], 2)
    far = swap(pair, "gx", True)
    pair = side(low_x, join([far, pair], 1), join([pair, far], 1))
    near = swap(pair, "gx", False)
    pair = side(low_x, join([pair, near], 1), join([near, pair], 1))

    row = lax.broadcasted_iota(jnp.int32, (24, 128), 0)
    edges = side(low_y, row == 23, row == 7), side(low_y, row == 0, row == 8)
    middle, pair = call(
        box_kernel,
        [(8, 24, 128), (2, 16, 24, 128)],
        [(2, 16, 48, 128), (3, 16, 48, 128)]
        + [(16, 48, 128)] * 3
        + [(2, 4, 48, 128), (2, 96, 128)]
        + [(3, 6, 24, 128), (4, 6, 24, 128), (6, 24, 128), (4, 48, 128)],
        pair,
        jnp.stack([jnp.where(edge, 0.0, 1.0) for edge in edges]),
        odd_z,
    )

    pair = side(low_x, pair[:, :12], pair[:, 4:])
    (filled,) = call(face_kernel, [(4, 12, 24, 128)], [], pair)
    far = swap(side(low_x, middle[:4], middle[4:]), "gx", True)
    middle = side(low_x, join([far, middle], 0), join([middle, far], 0))

    (pressure,) = call(
        last_kernel,
        [(8, 32, 128)],
        [(3, 12, *plane), (2, 12, *plane), (12, 24, 128), (192, 128), (16, 48, 128)],
        middle,
        pair,
        filled,
        kept,
    )
    return pressure


def solution(mesh):
    spec = P("gx", "gy", "gz")
    return jax.shard_map(local, mesh=mesh, in_specs=(spec, spec), out_specs=spec, check_vma=False)
```

```python
import math

import jax
import jax.numpy as jnp
from jax import lax
from jax.experimental import pallas as pl
from jax.experimental.pallas import tpu as pltpu
from jax.sharding import PartitionSpec as P

spectrum_top = 1.9
spectrum_low = 0.475
mean_value = (spectrum_top + spectrum_low) / 2
half_range = (spectrum_top - spectrum_low) / 2
omega_first = 1.0 / (mean_value + half_range * math.cos(math.pi / 4))
omega_second = 1.0 / (mean_value + half_range * math.cos(3 * math.pi / 4))
HIGHEST = lax.Precision.HIGHEST


def swap(block, axis, outer):
    count = lax.axis_size(axis)
    route = []
    for low in range(1 if outer else 0, count - 1, 2):
        route += [(low, low + 1), (low + 1, low)]
    return lax.ppermute(block, axis, route)


def shift(block, axis, step):
    count = lax.axis_size(axis)
    return lax.ppermute(block, axis, [(i, i + step) for i in range(count) if 0 <= i + step < count])


def cut(values, start, stop, dim):
    return lax.slice_in_dim(values, start, stop, axis=dim)


def join(pieces, dim):
    return jnp.concatenate(pieces, axis=dim)


def turn(plane, dim, step):
    return pltpu.roll(plane, -step % plane.shape[dim], dim)


class Operator:
    def __init__(self, faces):
        self.faces = faces

    def build(self, coeff, start, stop, take):
        before = coeff(start - 1) + coeff(start)
        self.faces[0, start - 1] = before
        for i in range(start, stop):
            here = coeff(i)
            across = here + coeff(i + 1)
            rows = here + turn(here, 0, 1)
            lanes = here + turn(here, 1, 1)
            for place, face in enumerate((across, rows, lanes)):
                self.faces[place, i] = face
            if take is not None:
                diagonal = (across + before) + (rows + turn(rows, 0, -1)) + (lanes + turn(lanes, 1, -1))
                take(i, jnp.where(here > 0, 1.0 / diagonal, 0.0))
            before = across

    def apply(self, field, start, stop, take):
        before = self.faces[0, start - 1] * (field(start - 1) - field(start))
        for i in range(start, stop):
            here = field(i)
            across = self.faces[0, i] * (here - field(i + 1))
            rows = self.faces[1, i] * (here - turn(here, 0, 1))
            lanes = self.faces[2, i] * (here - turn(here, 1, 1))
            take(i, (across - before) + (rows - turn(rows, 0, -1)) + (lanes - turn(lanes, 1, -1)))
            before = across


def sweep(operator, field, inverse, rhs, omega, start, stop, store):
    def take(i, applied):
        store(i, field(i) + (omega * (rhs(i) - applied)) * inverse(i))

    operator.apply(field, start, stop, take)


class BoxOperator:
    def __init__(self, upper, lower, faces):
        self.upper = upper
        self.lower = lower
        self.faces = faces

    def build(self, coeff, start, stop, take):
        before = coeff(start - 1) + coeff(start)
        self.faces[0, start - 1] = before
        for i in range(start, stop):
            here = coeff(i)
            across = here + coeff(i + 1)
            rows = here + self.upper * turn(here, 0, 1)
            back = here + self.lower * turn(here, 0, -1)
            lanes = here + turn(here, 1, 1)
            for place, face in enumerate((across, rows, lanes, back)):
                self.faces[place, i] = face
            diagonal = (across + before) + (rows + back) + (lanes + turn(lanes, 1, -1))
            take(i, jnp.where(here > 0, 1.0 / diagonal, 0.0))
            before = across

    def apply(self, field, start, stop, take):
        before = self.faces[0, start - 1] * (field(start - 1) - field(start))
        for i in range(start, stop):
            here = field(i)
            across = self.faces[0, i] * (here - field(i + 1))
            rows = self.faces[1, i] * (here - self.upper * turn(here, 0, 1))
            back = self.faces[3, i] * (here - self.lower * turn(here, 0, -1))
            lanes = self.faces[2, i] * (here - turn(here, 1, 1))
            take(i, (across - before) + (rows + back) + (lanes - turn(lanes, 1, -1)))
            before = across


def plane_of(ref, *lead):
    return lambda i: ref[(*lead, i)]


def keep_in(ref, *lead):
    def store(i, value):
        ref[(*lead, i)] = value

    return store


def halve_circular(plane, slot, weights):
    count = plane.shape[0] // 2
    slot[...] = plane
    even = slot[pl.ds(0, count, 2), :]
    odd = slot[pl.ds(1, count, 2), :]
    if not weights:
        return even + odd
    return 0.375 * (even + odd) + 0.125 * (turn(odd, 0, -1) + turn(even, 0, 1))


def halve_own(plane, slot, weights):
    slot[0:8] = plane[32:40]
    slot[8:40] = plane[0:32]
    slot[40:48] = plane[32:40]
    even = slot[pl.ds(8, 16, 2), :]
    odd = slot[pl.ds(9, 16, 2), :]
    if not weights:
        return even + odd
    return 0.375 * (even + odd) + 0.125 * (slot[pl.ds(7, 16, 2), :] + slot[pl.ds(10, 16, 2), :])


def near_rows(plane, own):
    row = lax.broadcasted_iota(jnp.int32, (8, plane.shape[1]), 0)
    edge = jnp.where(row < 4, plane[own : own + 8], plane[plane.shape[0] - 8 :])
    return jnp.concatenate([plane[:own], edge], axis=0)


def product(values, matrix):
    return jnp.dot(values, matrix, precision=HIGHEST, preferred_element_type=jnp.float32)


def lane_map(rows, columns, entries):
    row = lax.broadcasted_iota(jnp.int32, (rows, columns), 0)
    column = lax.broadcasted_iota(jnp.int32, (rows, columns), 1)
    return entries(row, column).astype(jnp.float32)


def signed(index, size, after):
    return jnp.where(index < after, index, index - size)


def gather_weights(fine, coarse):
    step = fine - 2 * coarse
    return jnp.where((step == 0) | (step == 1), 0.375, jnp.where((step == -1) | (step == 2), 0.125, 0.0))


def mean_weights(fine, coarse):
    step = fine - 2 * coarse
    return jnp.where((step == 0) | (step == 1), 0.5, 0.0)


def spread_weights(coarse, fine):
    step = fine - 2 * coarse
    return jnp.where((step == 0) | (step == 1), 0.75, jnp.where((step == -1) | (step == 2), 0.25, 0.0))


def fine_lane(f):
    return signed(f, 256, 192)


def middle_lane(m):
    return signed(m, 128, 96)


def coarse_lane(lane, odd):
    after = jnp.where(lane < 32, lane, jnp.where((lane == 32) & (odd == 1), 4096, lane - odd))
    before = jnp.where((lane == 127) & (odd == 0), 4096, lane - 127 - odd)
    return jnp.where(lane < 64, after, before)


def same_box(coarse, middle, odd):
    edge = 32 * odd
    return (coarse >= edge) == (middle >= 2 * edge)


def between(plane, at):
    return 0.375 * (plane(at) + plane(at + 1)) + 0.125 * (plane(at - 1) + plane(at + 2))


def both(plane, at):
    return plane(at) + plane(at + 1)


def restrict_level(weights, plane, first, halve, rows, piece, packed, matrix, store):
    lanes = piece.shape[2]
    parts = packed.shape[1] // lanes
    for j in range(4):
        value = (between if weights else both)(plane, first + 2 * j)
        for part in range(parts):
            packed[pl.ds(rows * j, rows), pl.ds(lanes * part, lanes)] = halve(
                value[:, lanes * part : lanes * part + lanes], piece.at[j * parts + part], weights
            )
    result = product(packed[...], matrix)
    for j in range(4):
        store(j, result[rows * j : rows * j + rows])


class Joined:
    def __init__(self, own, scratch, first, last, start):
        self.own = own
        self.scratch = scratch
        self.planes = first, last, start

    def __getitem__(self, place):
        first, last, start = self.planes
        lead, i = place[:-1], place[-1]
        return self.own[(*lead, i - start)] if first <= i <= last else self.scratch[place]

    def __setitem__(self, place, value):
        self.scratch[place] = value


def halo_edge():
    lane = lax.broadcasted_iota(jnp.int32, (40, 128), 1)
    return (lane < 32) | (lane >= 96)


def stage(cells, rhs, coeff, i):
    edge = halo_edge()
    rhs[i, :, 0:128] = 2.0 * cells[0, i]
    rhs[i, :, 128:256] = jnp.where(edge, 2.0 * cells[2, i], 0.0)
    coeff[i, :, 0:128] = cells[1, i]
    coeff[i, :, 128:256] = jnp.where(edge, pltpu.roll(cells[2, i], 64, 1), 0.0)


def own_kernel(cells, faces, inverse, pre, left, middle_coeff, rhs, coeff, field, piece, packed):
    for i in range(8):
        stage(cells, rhs, coeff, i)
    operator = Operator(faces)

    def begin(i, value):
        inverse[i] = value
        field[i] = omega_first * rhs[i] * value

    operator.build(plane_of(coeff), 1, 7, begin)

    def store_pre(i, value):
        pre[i - 2] = value

    sweep(operator, plane_of(field), plane_of(inverse), plane_of(rhs), omega_second, 2, 6, store_pre)

    def leave(i, applied):
        left[i - 3] = jnp.where(coeff[i] > 0, rhs[i] - applied, 0.0)

    operator.apply(lambda i: pre[i - 2], 3, 5, leave)
    matrix = lane_map(256, 128, lambda f, c: 0.25 * mean_weights(fine_lane(f), middle_lane(c)))
    restrict_level(
        False, plane_of(coeff), 0, halve_own, 16, piece, packed, matrix, keep_in(middle_coeff)
    )


def fine_kernel(
    wide, own_faces, own_inverse, own_pre, own_left, own_coeff,
    pair, low, high, kept, faces, inverse, rhs, coeff, field, pre, left, piece, packed,
):
    for i in range(16):
        stage(wide, rhs, coeff, i)
    operator = Operator(Joined(own_faces, faces, 5, 10, 4))
    for start in (1, 11):
        operator.build(plane_of(coeff), start, start + 4, keep_in(inverse))
    inverses = plane_of(Joined(own_inverse, inverse, 5, 10, 4))
    smoothed = plane_of(Joined(own_pre, pre, 6, 9, 6))
    leftover = plane_of(Joined(own_left, left, 7, 8, 7))
    for i in (*range(1, 7), *range(9, 15)):
        field[i] = omega_first * rhs[i] * inverses(i)
    for start in (2, 10):
        sweep(
            operator, plane_of(field), inverses, plane_of(rhs), omega_second, start, start + 4, keep_in(pre)
        )
    for i in range(2, 14):
        for kind, plane in enumerate((plane_of(coeff), plane_of(rhs), smoothed, inverses)):
            kept[kind, i - 2] = plane(i)

    def leave(i, applied):
        left[i] = jnp.where(coeff[i] > 0, rhs[i] - applied, 0.0)

    for start in (3, 9):
        operator.apply(smoothed, start, start + 4, leave)
    matrix = lane_map(256, 128, lambda f, c: 4.0 * gather_weights(fine_lane(f), middle_lane(c)))
    restrict_level(True, leftover, 4, halve_own, 16, piece, packed, matrix, keep_in(pair, 0))
    for j in range(4):
        pair[1, j] = own_coeff[j]
    for kind in range(2):
        for j in range(4):
            low[kind, j] = pair[kind, j, 0:12]
            high[kind, j] = pair[kind, j, 4:16]


def box_kernel(narrow, box, parity, corrected, kept, pair, faces, inverse, field, other, piece, packed, low, low_faces, low_inverse, risen):
    after = lax.broadcasted_iota(jnp.int32, (8, 128), 0) < 4
    for kind in range(2):
        for i in range(16):
            pair[kind, i, 0:24] = narrow[kind, i, 0:24]
            pair[kind, i, 24:32] = jnp.where(after, narrow[kind, i, 24:32], 0.0)
            pair[kind, i, 32:40] = jnp.where(after, 0.0, narrow[kind, i, 24:32])
            pair[kind, i, 40:48] = narrow[kind, i, 32:40]
    rhs, coeff = plane_of(pair, 0), plane_of(pair, 1)
    operator = Operator(faces)

    def begin(i, value):
        inverse[i] = value
        field[i] = omega_first * rhs(i) * value

    operator.build(coeff, 1, 15, begin)
    sweep(operator, plane_of(field), plane_of(inverse), rhs, omega_second, 2, 14, keep_in(other))

    def leave(i, applied):
        field[i] = jnp.where(coeff(i) > 0, rhs(i) - applied, 0.0)

    operator.apply(plane_of(other), 3, 13, leave)
    odd = parity[0]
    for kind, matrix in enumerate(
        (
            lane_map(128, 128, lambda m, c: 4.0 * gather_weights(middle_lane(m), coarse_lane(c, odd))),
            lane_map(128, 128, lambda m, c: 0.25 * mean_weights(middle_lane(m), coarse_lane(c, odd))),
        )
    ):

        def store(j, value, kind=kind):
            low[kind, j + 1] = value

        plane = coeff if kind else plane_of(field)
        restrict_level(kind == 0, plane, 4, halve_circular, 24, piece.at[kind], packed.at[kind], matrix, store)
    for place in (0, 5):
        for kind in range(3):
            low[kind, place] = jnp.zeros((24, 128), jnp.float32)
    upper, lower = box[0], box[1]
    coarse = BoxOperator(upper, lower, low_faces)

    def begin_low(i, value):
        low_inverse[i] = value
        low[2, i] = omega_first * low[0, i] * value

    coarse.build(plane_of(low, 1), 1, 5, begin_low)

    def store_low(i, value):
        packed[0, pl.ds(24 * (i - 1), 24), :] = value

    sweep(coarse, plane_of(low, 2), plane_of(low_inverse), plane_of(low, 0), omega_second, 1, 5, store_low)

    def spread_box(c, m):
        coarse, fine = coarse_lane(c, odd), middle_lane(m)
        return jnp.where(same_box(coarse, fine, odd), spread_weights(coarse, fine), 0.0)

    result = product(packed[0], lane_map(128, 128, spread_box))
    for j in range(4):
        spread_rows(result[24 * j : 24 * j + 24], risen.at[j], upper, lower)
    for i in range(8):
        value = 0.75 * risen[i // 2]
        near = i // 2 + (1 if i % 2 else -1)
        if 0 <= near < 4:
            value = value + 0.25 * risen[near]
        corrected[i] = near_rows(other[i + 4] + value, 16)
    for kind in range(2):
        for i in range(16):
            kept[kind, i] = near_rows(pair[kind, i], 16)


def spread_rows(values, target, upper=1.0, lower=1.0):
    count = values.shape[0]
    target[pl.ds(0, count, 2), :] = 0.75 * values + 0.25 * (lower * turn(values, 0, -1))
    target[pl.ds(1, count, 2), :] = 0.75 * values + 0.25 * (upper * turn(values, 0, 1))


def face_kernel(pair, filled):
    def take(i, value):
        filled[3, i] = value

    Operator(filled).build(plane_of(pair, 1), 1, 11, take)


def last_kernel(middle, pair, filled, kept, out, faces, field, field_m, packed, risen):
    operator = Operator(filled)
    rhs_m, at_m = plane_of(pair, 0), plane_of(filled, 3)
    sweep(operator, plane_of(middle), at_m, rhs_m, omega_first, 1, 11, keep_in(field_m))

    def store_packed(i, value):
        packed[pl.ds(24 * (i - 2), 24), :] = value

    sweep(operator, plane_of(field_m), at_m, rhs_m, omega_second, 2, 10, store_packed)
    result = product(
        packed[...], lane_map(128, 256, lambda c, f: spread_weights(middle_lane(c), fine_lane(f)))
    )
    for place in range(8):
        for half in range(2):
            spread_rows(
                result[24 * place : 24 * place + 24, 128 * half : 128 * half + 128],
                risen.at[2 * place + half],
            )

    def lifted(place):
        halves = [
            near_rows(risen[2 * place + half], 32) for half in range(2)
        ]
        return jnp.concatenate(halves, axis=1)

    fine = Operator(faces)
    coeff, rhs = plane_of(kept, 0), plane_of(kept, 1)
    fine.build(coeff, 1, 11, None)
    inverse = plane_of(kept, 3)
    for i in range(12):
        place = i // 2 + 1
        value = 0.75 * lifted(place) + 0.25 * lifted(place + (1 if i % 2 else -1))
        field[0, i] = kept[2, i] + jnp.where(coeff(i) > 0, value, 0.0)
    sweep(fine, plane_of(field, 0), inverse, rhs, omega_first, 1, 11, keep_in(field, 1))

    def store_out(i, value):
        out[i - 2] = value[:32, :128]

    sweep(fine, plane_of(field, 1), inverse, rhs, omega_second, 2, 10, store_out)


interpret = False
VMEM = pl.BlockSpec(memory_space=pltpu.VMEM)
SMEM = pl.BlockSpec(memory_space=pltpu.SMEM)
HBM = pl.BlockSpec(memory_space=pltpu.HBM)


def call(kernel, outs, scratch, *arguments, specs=None):
    return pl.pallas_call(
        kernel,
        out_shape=[jax.ShapeDtypeStruct(shape, jnp.float32) for shape in outs],
        in_specs=specs or [VMEM if value.ndim > 1 else SMEM for value in arguments],
        out_specs=[VMEM] * len(outs),
        scratch_shapes=[
            pltpu.VMEM(shape, jnp.float32) if isinstance(shape, tuple) else shape for shape in scratch
        ],
        compiler_params=pltpu.CompilerParams(vmem_limit_bytes=24 * 1024 * 1024),
        interpret=interpret,
    )(*arguments)


def take_lanes(values, matrix):
    rows = values.reshape(-1, values.shape[-1])
    return lax.dot_general(matrix, rows, (((0,), (1,)), ((), ())), precision=HIGHEST)


def put_lanes(strip, matrix, shape):
    rows = lax.dot_general(strip, matrix, (((0,), (0,)), ((), ())), precision=HIGHEST)
    return rows.reshape(shape)


def local(source, conductivity):
    low_x = lax.axis_index("gx") % 2 == 0
    low_y = lax.axis_index("gy") % 2 == 0
    odd_z = (lax.axis_index("gz") % 2).reshape(1)

    def side(low, when_low, when_high):
        return jnp.where(low, when_low, when_high)

    cells = jnp.stack([source, conductivity])
    low, high = cells[:, :, :4], cells[:, :, 28:]
    cells = lax.optimization_barrier(cells)
    cells = join([cells, shift(low, "gy", -1), shift(high, "gy", 1)], 2)

    strips = take_lanes(cells, lane_map(128, 64, lambda z, k: z == k + jnp.where(k < 32, 0, 64)))
    after = shift(strips[:32], "gz", -1)
    before = shift(strips[32:], "gz", 1)
    rows = strips.shape[1] // 2
    halo = join([after[:, :rows], before[:, rows:], after[:, rows:], before[:, :rows]], 0)
    halo = put_lanes(halo, lane_map(128, 128, lambda k, z: k == z), (1, 8, 40, 128))
    cells = join([cells, halo], 0)

    plane = (40, 256)
    own = call(
        own_kernel,
        [(3, 8, *plane), (8, *plane), (4, *plane), (2, *plane), (4, 16, 128)],
        [(8, *plane), (8, *plane), (8, *plane), (8, 48, 128), (64, 256)],
        cells,
    )
    far = swap(side(low_x, cells[:, :4], cells[:, 4:]), "gx", True)
    near = swap(side(low_x, cells[:, 4:], cells[:, :4]), "gx", False)
    wide = join([side(low_x, far, near), cells, side(low_x, near, far)], 1)

    pair, low, high, kept = call(
        fine_kernel,
        [(2, 4, 16, 128), (2, 4, 12, 128), (2, 4, 12, 128), (4, 12, *plane)],
        [(3, 16, *plane)] + [(16, *plane)] * 6 + [(8, 48, 128), (64, 256)],
        wide,
        *own,
    )

    pair = join([pair, shift(low, "gy", -1), shift(high, "gy", 1)], 2)
    far = swap(pair, "gx", True)
    pair = side(low_x, join([far, pair], 1), join([pair, far], 1))
    near = swap(pair, "gx", False)
    pair = side(low_x, join([pair, near], 1), join([near, pair], 1))

    row = lax.broadcasted_iota(jnp.int32, (24, 128), 0)
    edges = side(low_y, row == 23, row == 7), side(low_y, row == 0, row == 8)
    middle, pair = call(
        box_kernel,
        [(8, 24, 128), (2, 16, 24, 128)],
        [(2, 16, 48, 128), (3, 16, 48, 128)]
        + [(16, 48, 128)] * 3
        + [(2, 4, 48, 128), (2, 96, 128)]
        + [(3, 6, 24, 128), (4, 6, 24, 128), (6, 24, 128), (4, 48, 128)],
        pair,
        jnp.stack([jnp.where(edge, 0.0, 1.0) for edge in edges]),
        odd_z,
    )

    pair = side(low_x, pair[:, :12], pair[:, 4:])
    (filled,) = call(face_kernel, [(4, 12, 24, 128)], [], pair)
    far = swap(side(low_x, middle[:4], middle[4:]), "gx", True)
    middle = side(low_x, join([far, middle], 0), join([middle, far], 0))

    (pressure,) = call(
        last_kernel,
        [(8, 32, 128)],
        [(3, 12, *plane), (2, 12, *plane), (12, 24, 128), (192, 128), (16, 48, 128)],
        middle,
        pair,
        filled,
        kept,
    )
    return pressure


def solution(mesh):
    spec = P("gx", "gy", "gz")
    return jax.shard_map(local, mesh=mesh, in_specs=(spec, spec), out_specs=spec, check_vma=False)
```

```python
import math

import jax
import jax.numpy as jnp
from jax import lax
from jax.experimental import pallas as pl
from jax.experimental.pallas import tpu as pltpu
from jax.sharding import PartitionSpec as P

spectrum_top = 1.9
spectrum_low = 0.475
mean_value = (spectrum_top + spectrum_low) / 2
half_range = (spectrum_top - spectrum_low) / 2
omega_first = 1.0 / (mean_value + half_range * math.cos(math.pi / 4))
omega_second = 1.0 / (mean_value + half_range * math.cos(3 * math.pi / 4))
HIGHEST = lax.Precision.HIGHEST


def swap(block, axis, outer):
    count = lax.axis_size(axis)
    route = []
    for low in range(1 if outer else 0, count - 1, 2):
        route += [(low, low + 1), (low + 1, low)]
    return lax.ppermute(block, axis, route)


def shift(block, axis, step):
    count = lax.axis_size(axis)
    return lax.ppermute(block, axis, [(i, i + step) for i in range(count) if 0 <= i + step < count])


def join(pieces, dim):
    return jnp.concatenate(pieces, axis=dim)


def turn(plane, dim, step):
    return pltpu.roll(plane, -step % plane.shape[dim], dim)


class Operator:
    def __init__(self, faces):
        self.faces = faces

    def build(self, coeff, start, stop, take):
        before = coeff(start - 1) + coeff(start)
        self.faces[0, start - 1] = before
        for i in range(start, stop):
            here = coeff(i)
            across = here + coeff(i + 1)
            rows = here + turn(here, 0, 1)
            lanes = here + turn(here, 1, 1)
            for place, face in enumerate((across, rows, lanes)):
                self.faces[place, i] = face
            if take is not None:
                diagonal = (across + before) + (rows + turn(rows, 0, -1)) + (lanes + turn(lanes, 1, -1))
                take(i, jnp.where(here > 0, 1.0 / diagonal, 0.0))
            before = across

    def apply(self, field, start, stop, take):
        before = self.faces[0, start - 1] * (field(start - 1) - field(start))
        for i in range(start, stop):
            here = field(i)
            across = self.faces[0, i] * (here - field(i + 1))
            rows = self.faces[1, i] * (here - turn(here, 0, 1))
            lanes = self.faces[2, i] * (here - turn(here, 1, 1))
            take(i, (across - before) + (rows - turn(rows, 0, -1)) + (lanes - turn(lanes, 1, -1)))
            before = across


def sweep(operator, field, inverse, rhs, omega, start, stop, store):
    def take(i, applied):
        store(i, field(i) + (omega * (rhs(i) - applied)) * inverse(i))

    operator.apply(field, start, stop, take)


class BoxOperator:
    def __init__(self, upper, lower, faces):
        self.upper = upper
        self.lower = lower
        self.faces = faces

    def build(self, coeff, start, stop, take):
        before = coeff(start - 1) + coeff(start)
        self.faces[0, start - 1] = before
        for i in range(start, stop):
            here = coeff(i)
            across = here + coeff(i + 1)
            rows = here + self.upper * turn(here, 0, 1)
            back = here + self.lower * turn(here, 0, -1)
            lanes = here + turn(here, 1, 1)
            for place, face in enumerate((across, rows, lanes, back)):
                self.faces[place, i] = face
            diagonal = (across + before) + (rows + back) + (lanes + turn(lanes, 1, -1))
            take(i, jnp.where(here > 0, 1.0 / diagonal, 0.0))
            before = across

    def apply(self, field, start, stop, take):
        before = self.faces[0, start - 1] * (field(start - 1) - field(start))
        for i in range(start, stop):
            here = field(i)
            across = self.faces[0, i] * (here - field(i + 1))
            rows = self.faces[1, i] * (here - self.upper * turn(here, 0, 1))
            back = self.faces[3, i] * (here - self.lower * turn(here, 0, -1))
            lanes = self.faces[2, i] * (here - turn(here, 1, 1))
            take(i, (across - before) + (rows + back) + (lanes - turn(lanes, 1, -1)))
            before = across


def plane_of(ref, *lead):
    return lambda i: ref[(*lead, i)]


def keep_in(ref, *lead):
    def store(i, value):
        ref[(*lead, i)] = value

    return store


def halve_circular(plane, slot, weights):
    count = plane.shape[0] // 2
    slot[...] = plane
    even = slot[pl.ds(0, count, 2), :]
    odd = slot[pl.ds(1, count, 2), :]
    if not weights:
        return even + odd
    return 0.375 * (even + odd) + 0.125 * (turn(odd, 0, -1) + turn(even, 0, 1))


def halve_own(plane, slot, weights):
    slot[0:8] = plane[32:40]
    slot[8:40] = plane[0:32]
    slot[40:48] = plane[32:40]
    even = slot[pl.ds(8, 16, 2), :]
    odd = slot[pl.ds(9, 16, 2), :]
    if not weights:
        return even + odd
    return 0.375 * (even + odd) + 0.125 * (slot[pl.ds(7, 16, 2), :] + slot[pl.ds(10, 16, 2), :])


def near_rows(plane, own):
    row = lax.broadcasted_iota(jnp.int32, (8, plane.shape[1]), 0)
    edge = jnp.where(row < 4, plane[own : own + 8], plane[plane.shape[0] - 8 :])
    return jnp.concatenate([plane[:own], edge], axis=0)


def product(values, matrix):
    return jnp.dot(values, matrix, precision=HIGHEST, preferred_element_type=jnp.float32)


def lane_map(rows, columns, entries):
    row = lax.broadcasted_iota(jnp.int32, (rows, columns), 0)
    column = lax.broadcasted_iota(jnp.int32, (rows, columns), 1)
    return entries(row, column).astype(jnp.float32)


def signed(index, size, after):
    return jnp.where(index < after, index, index - size)


def gather_weights(fine, coarse):
    step = fine - 2 * coarse
    return jnp.where((step == 0) | (step == 1), 0.375, jnp.where((step == -1) | (step == 2), 0.125, 0.0))


def mean_weights(fine, coarse):
    step = fine - 2 * coarse
    return jnp.where((step == 0) | (step == 1), 0.5, 0.0)


def spread_weights(coarse, fine):
    step = fine - 2 * coarse
    return jnp.where((step == 0) | (step == 1), 0.75, jnp.where((step == -1) | (step == 2), 0.25, 0.0))


def fine_lane(f):
    return signed(f, 256, 192)


def middle_lane(m):
    return signed(m, 128, 96)


def coarse_lane(lane, odd):
    after = jnp.where(lane < 32, lane, jnp.where((lane == 32) & (odd == 1), 4096, lane - odd))
    before = jnp.where((lane == 127) & (odd == 0), 4096, lane - 127 - odd)
    return jnp.where(lane < 64, after, before)


def same_box(coarse, middle, odd):
    edge = 32 * odd
    return (coarse >= edge) == (middle >= 2 * edge)


def between(plane, at):
    return 0.375 * (plane(at) + plane(at + 1)) + 0.125 * (plane(at - 1) + plane(at + 2))


def both(plane, at):
    return plane(at) + plane(at + 1)


def restrict_level(weights, plane, first, halve, rows, piece, packed, matrix, store):
    lanes = piece.shape[2]
    parts = packed.shape[1] // lanes
    for j in range(4):
        value = (between if weights else both)(plane, first + 2 * j)
        for part in range(parts):
            packed[pl.ds(rows * j, rows), pl.ds(lanes * part, lanes)] = halve(
                value[:, lanes * part : lanes * part + lanes], piece.at[j * parts + part], weights
            )
    result = product(packed[...], matrix)
    for j in range(4):
        store(j, result[rows * j : rows * j + rows])


class Joined:
    def __init__(self, own, scratch, first, last, start):
        self.own = own
        self.scratch = scratch
        self.planes = first, last, start

    def __getitem__(self, place):
        first, last, start = self.planes
        lead, i = place[:-1], place[-1]
        return self.own[(*lead, i - start)] if first <= i <= last else self.scratch[place]

    def __setitem__(self, place, value):
        self.scratch[place] = value


def halo_edge():
    lane = lax.broadcasted_iota(jnp.int32, (40, 128), 1)
    return (lane < 32) | (lane >= 96)


def stage(cells, rhs, coeff, i):
    edge = halo_edge()
    rhs[i, :, 0:128] = 2.0 * cells[0, i]
    rhs[i, :, 128:256] = jnp.where(edge, 2.0 * cells[2, i], 0.0)
    coeff[i, :, 0:128] = cells[1, i]
    coeff[i, :, 128:256] = jnp.where(edge, pltpu.roll(cells[2, i], 64, 1), 0.0)


def own_kernel(cells, faces, inverse, pre, left, middle_coeff, rhs, coeff, field, piece, packed):
    for i in range(8):
        stage(cells, rhs, coeff, i)
    operator = Operator(faces)

    def begin(i, value):
        inverse[i] = value
        field[i] = omega_first * rhs[i] * value

    operator.build(plane_of(coeff), 1, 7, begin)

    def store_pre(i, value):
        pre[i - 2] = value

    sweep(operator, plane_of(field), plane_of(inverse), plane_of(rhs), omega_second, 2, 6, store_pre)

    def leave(i, applied):
        left[i - 3] = jnp.where(coeff[i] > 0, rhs[i] - applied, 0.0)

    operator.apply(lambda i: pre[i - 2], 3, 5, leave)
    matrix = lane_map(256, 128, lambda f, c: 0.25 * mean_weights(fine_lane(f), middle_lane(c)))
    restrict_level(
        False, plane_of(coeff), 0, halve_own, 16, piece, packed, matrix, keep_in(middle_coeff)
    )


def fine_kernel(
    wide, own_faces, own_inverse, own_pre, own_left, own_coeff,
    pair, low, high, kept, faces, inverse, rhs, coeff, field, pre, left, piece, packed,
):
    for i in range(16):
        stage(wide, rhs, coeff, i)
    operator = Operator(Joined(own_faces, faces, 5, 10, 4))
    for start in (1, 11):
        operator.build(plane_of(coeff), start, start + 4, keep_in(inverse))
    inverses = plane_of(Joined(own_inverse, inverse, 5, 10, 4))
    smoothed = plane_of(Joined(own_pre, pre, 6, 9, 6))
    leftover = plane_of(Joined(own_left, left, 7, 8, 7))
    for i in (*range(1, 7), *range(9, 15)):
        field[i] = omega_first * rhs[i] * inverses(i)
    for start in (2, 10):
        sweep(
            operator, plane_of(field), inverses, plane_of(rhs), omega_second, start, start + 4, keep_in(pre)
        )
    for i in range(2, 14):
        for kind, plane in enumerate((plane_of(coeff), plane_of(rhs), smoothed, inverses)):
            kept[kind, i - 2] = plane(i)

    def leave(i, applied):
        left[i] = jnp.where(coeff[i] > 0, rhs[i] - applied, 0.0)

    for start in (3, 9):
        operator.apply(smoothed, start, start + 4, leave)
    matrix = lane_map(256, 128, lambda f, c: 4.0 * gather_weights(fine_lane(f), middle_lane(c)))
    restrict_level(True, leftover, 4, halve_own, 16, piece, packed, matrix, keep_in(pair, 0))
    for j in range(4):
        pair[1, j] = own_coeff[j]
    for kind in range(2):
        for j in range(4):
            low[kind, j] = pair[kind, j, 0:12]
            high[kind, j] = pair[kind, j, 4:16]


def box_kernel(narrow, box, parity, corrected, kept, pair, faces, inverse, field, other, piece, packed, low, low_faces, low_inverse, risen):
    after = lax.broadcasted_iota(jnp.int32, (8, 128), 0) < 4
    for kind in range(2):
        for i in range(16):
            pair[kind, i, 0:24] = narrow[kind, i, 0:24]
            pair[kind, i, 24:32] = jnp.where(after, narrow[kind, i, 24:32], 0.0)
            pair[kind, i, 32:40] = jnp.where(after, 0.0, narrow[kind, i, 24:32])
            pair[kind, i, 40:48] = narrow[kind, i, 32:40]
    rhs, coeff = plane_of(pair, 0), plane_of(pair, 1)
    operator = Operator(faces)

    def begin(i, value):
        inverse[i] = value
        field[i] = omega_first * rhs(i) * value

    operator.build(coeff, 1, 15, begin)
    sweep(operator, plane_of(field), plane_of(inverse), rhs, omega_second, 2, 14, keep_in(other))

    def leave(i, applied):
        field[i] = jnp.where(coeff(i) > 0, rhs(i) - applied, 0.0)

    operator.apply(plane_of(other), 3, 13, leave)
    odd = parity[0]
    for kind, matrix in enumerate(
        (
            lane_map(128, 128, lambda m, c: 4.0 * gather_weights(middle_lane(m), coarse_lane(c, odd))),
            lane_map(128, 128, lambda m, c: 0.25 * mean_weights(middle_lane(m), coarse_lane(c, odd))),
        )
    ):

        def store(j, value, kind=kind):
            low[kind, j + 1] = value

        plane = coeff if kind else plane_of(field)
        restrict_level(kind == 0, plane, 4, halve_circular, 24, piece.at[kind], packed.at[kind], matrix, store)
    for place in (0, 5):
        for kind in range(3):
            low[kind, place] = jnp.zeros((24, 128), jnp.float32)
    upper, lower = box[0], box[1]
    coarse = BoxOperator(upper, lower, low_faces)

    def begin_low(i, value):
        low_inverse[i] = value
        low[2, i] = omega_first * low[0, i] * value

    coarse.build(plane_of(low, 1), 1, 5, begin_low)

    def store_low(i, value):
        packed[0, pl.ds(24 * (i - 1), 24), :] = value

    sweep(coarse, plane_of(low, 2), plane_of(low_inverse), plane_of(low, 0), omega_second, 1, 5, store_low)

    def spread_box(c, m):
        coarse, fine = coarse_lane(c, odd), middle_lane(m)
        return jnp.where(same_box(coarse, fine, odd), spread_weights(coarse, fine), 0.0)

    result = product(packed[0], lane_map(128, 128, spread_box))
    for j in range(4):
        spread_rows(result[24 * j : 24 * j + 24], risen.at[j], upper, lower)
    for i in range(8):
        value = 0.75 * risen[i // 2]
        near = i // 2 + (1 if i % 2 else -1)
        if 0 <= near < 4:
            value = value + 0.25 * risen[near]
        corrected[i] = near_rows(other[i + 4] + value, 16)
    for kind in range(2):
        for i in range(16):
            kept[kind, i] = near_rows(pair[kind, i], 16)


def spread_rows(values, target, upper=1.0, lower=1.0):
    count = values.shape[0]
    target[pl.ds(0, count, 2), :] = 0.75 * values + 0.25 * (lower * turn(values, 0, -1))
    target[pl.ds(1, count, 2), :] = 0.75 * values + 0.25 * (upper * turn(values, 0, 1))


def face_kernel(pair, filled):
    def take(i, value):
        filled[3, i] = value

    Operator(filled).build(plane_of(pair, 1), 1, 11, take)


def last_kernel(middle, pair, filled, kept, out, faces, field, field_m, packed, risen):
    operator = Operator(filled)
    rhs_m, at_m = plane_of(pair, 0), plane_of(filled, 3)
    sweep(operator, plane_of(middle), at_m, rhs_m, omega_first, 1, 11, keep_in(field_m))

    def store_packed(i, value):
        packed[pl.ds(24 * (i - 2), 24), :] = value

    sweep(operator, plane_of(field_m), at_m, rhs_m, omega_second, 2, 10, store_packed)
    result = product(
        packed[...], lane_map(128, 256, lambda c, f: spread_weights(middle_lane(c), fine_lane(f)))
    )
    for place in range(8):
        for half in range(2):
            spread_rows(
                result[24 * place : 24 * place + 24, 128 * half : 128 * half + 128],
                risen.at[2 * place + half],
            )

    def lifted(place):
        halves = [
            near_rows(risen[2 * place + half], 32) for half in range(2)
        ]
        return jnp.concatenate(halves, axis=1)

    fine = Operator(faces)
    coeff, rhs = plane_of(kept, 0), plane_of(kept, 1)
    fine.build(coeff, 1, 11, None)
    inverse = plane_of(kept, 3)
    for i in range(12):
        place = i // 2 + 1
        value = 0.75 * lifted(place) + 0.25 * lifted(place + (1 if i % 2 else -1))
        field[0, i] = kept[2, i] + jnp.where(coeff(i) > 0, value, 0.0)
    sweep(fine, plane_of(field, 0), inverse, rhs, omega_first, 1, 11, keep_in(field, 1))

    def store_out(i, value):
        out[i - 2] = value[:32, :128]

    sweep(fine, plane_of(field, 1), inverse, rhs, omega_second, 2, 10, store_out)


interpret = False
VMEM = pl.BlockSpec(memory_space=pltpu.VMEM)
SMEM = pl.BlockSpec(memory_space=pltpu.SMEM)
HBM = pl.BlockSpec(memory_space=pltpu.HBM)


def call(kernel, outs, scratch, *arguments, specs=None):
    return pl.pallas_call(
        kernel,
        out_shape=[jax.ShapeDtypeStruct(shape, jnp.float32) for shape in outs],
        in_specs=specs or [VMEM if value.ndim > 1 else SMEM for value in arguments],
        out_specs=[VMEM] * len(outs),
        scratch_shapes=[
            pltpu.VMEM(shape, jnp.float32) if isinstance(shape, tuple) else shape for shape in scratch
        ],
        compiler_params=pltpu.CompilerParams(vmem_limit_bytes=24 * 1024 * 1024),
        interpret=interpret,
    )(*arguments)


def take_lanes(values, matrix):
    rows = values.reshape(-1, values.shape[-1])
    return lax.dot_general(matrix, rows, (((0,), (1,)), ((), ())), precision=HIGHEST)


def put_lanes(strip, matrix, shape):
    rows = lax.dot_general(strip, matrix, (((0,), (0,)), ((), ())), precision=HIGHEST)
    return rows.reshape(shape)


def cycle(source, conductivity):
    low_x = lax.axis_index("gx") % 2 == 0
    low_y = lax.axis_index("gy") % 2 == 0
    odd_z = (lax.axis_index("gz") % 2).reshape(1)

    def side(low, when_low, when_high):
        return jnp.where(low, when_low, when_high)

    cells = jnp.stack([source, conductivity])
    low, high = cells[:, :, :4], cells[:, :, 28:]
    cells = lax.optimization_barrier(cells)
    cells = join([cells, shift(low, "gy", -1), shift(high, "gy", 1)], 2)

    strips = take_lanes(cells, lane_map(128, 64, lambda z, k: z == k + jnp.where(k < 32, 0, 64)))
    after = shift(strips[:32], "gz", -1)
    before = shift(strips[32:], "gz", 1)
    rows = strips.shape[1] // 2
    halo = join([after[:, :rows], before[:, rows:], after[:, rows:], before[:, :rows]], 0)
    halo = put_lanes(halo, lane_map(128, 128, lambda k, z: k == z), (1, 8, 40, 128))
    cells = join([cells, halo], 0)

    plane = (40, 256)
    own = call(
        own_kernel,
        [(3, 8, *plane), (8, *plane), (4, *plane), (2, *plane), (4, 16, 128)],
        [(8, *plane), (8, *plane), (8, *plane), (8, 48, 128), (64, 256)],
        cells,
    )
    far = swap(side(low_x, cells[:, :4], cells[:, 4:]), "gx", True)
    near = swap(side(low_x, cells[:, 4:], cells[:, :4]), "gx", False)
    wide = join([side(low_x, far, near), cells, side(low_x, near, far)], 1)

    pair, low, high, kept = call(
        fine_kernel,
        [(2, 4, 16, 128), (2, 4, 12, 128), (2, 4, 12, 128), (4, 12, *plane)],
        [(3, 16, *plane)] + [(16, *plane)] * 6 + [(8, 48, 128), (64, 256)],
        wide,
        *own,
    )

    pair = join([pair, shift(low, "gy", -1), shift(high, "gy", 1)], 2)
    far = swap(pair, "gx", True)
    pair = side(low_x, join([far, pair], 1), join([pair, far], 1))
    near = swap(pair, "gx", False)
    pair = side(low_x, join([pair, near], 1), join([near, pair], 1))

    row = lax.broadcasted_iota(jnp.int32, (24, 128), 0)
    edges = side(low_y, row == 23, row == 7), side(low_y, row == 0, row == 8)
    middle, pair = call(
        box_kernel,
        [(8, 24, 128), (2, 16, 24, 128)],
        [(2, 16, 48, 128), (3, 16, 48, 128)]
        + [(16, 48, 128)] * 3
        + [(2, 4, 48, 128), (2, 96, 128)]
        + [(3, 6, 24, 128), (4, 6, 24, 128), (6, 24, 128), (4, 48, 128)],
        pair,
        jnp.stack([jnp.where(edge, 0.0, 1.0) for edge in edges]),
        odd_z,
    )

    pair = side(low_x, pair[:, :12], pair[:, 4:])
    (filled,) = call(face_kernel, [(4, 12, 24, 128)], [], pair)
    far = swap(side(low_x, middle[:4], middle[4:]), "gx", True)
    middle = side(low_x, join([far, middle], 0), join([middle, far], 0))

    (pressure,) = call(
        last_kernel,
        [(8, 32, 128)],
        [(3, 12, *plane), (2, 12, *plane), (12, 24, 128), (192, 128), (16, 48, 128)],
        middle,
        pair,
        filled,
        kept,
    )
    return pressure


def solution(mesh):
    spec = P("gx", "gy", "gz")
    return jax.shard_map(cycle, mesh=mesh, in_specs=(spec, spec), out_specs=spec, check_vma=False)
```
